256 devices in a mesh: dp: 32 (over z, y), expert: 8 (over x, core).
Axes of the slice: x: 4, y: 4, z: 8, core: 2. Of those that a mesh axis runs over, the one named last changes fastest.
Arguments:
- tokens: bfloat16 [8192, 2048], P('dp'), may hold values from -6 to 6
- expert_ids: int32 [8192, 8], P('dp', 'expert'), may hold values from 0 to 127, as said below
- gates: float32 [8192, 8], P('dp', 'expert'), may hold values from 0.05 to 0.25
- positives: int32 [128], P('dp'), may hold values from 0 to 127, as said below
- gate_up: bfloat16 [256, 2048, 768], P(('dp', 'expert')), may hold values from -0.125 to 0.125
- down: bfloat16 [256, 384, 2048], P(('dp', 'expert')), may hold values from -0.21875 to 0.21875
Outputs:
- layer_out: bfloat16 [8192, 2048], P('dp')
- grad_gate_up: bfloat16 [256, 2048, 768], P(('dp', 'expert'))
- grad_down: bfloat16 [256, 384, 2048], P(('dp', 'expert'))
The draws below stay inside these ranges and needn't reach their ends.
Inputs may be any that keep to these rules, and one draw needn't show every extreme that they name: `expert_ids`: each row names 8 different experts. In the 256 rows of one index of dp no expert is named more than 4 times in one column, and in each column one expert is named exactly 4 times in the rows of every index of dp. positives[i] != i and positives[positives[i]] = i.
All inputs are finite; a program needn't handle non-finite values.
Results may differ from the reference program's by a relative error of at most 0.015.
Values may be sent and summed in bfloat16 or wider, within the bound.
A program may use at most 128 MiB of HBM per device.

```python
import jax
import jax.numpy as jnp
from jax import lax

D = 2048
FF = 768
TOPK = 8
TOK_DEV = 256
LENGTH = 64
EXPERTS = 128
SLICES = 256
HALF = 384
CAP = 4
TOKENS = 8192
SEQS = 128


def draw_expert_ids(key, part):
    base_key = jax.random.fold_in(key, 101)
    key_hot, key_offsets, key_blocks = jax.random.split(base_key, 3)
    hot_expert = jax.random.randint(key_hot, (), 0, EXPERTS).astype(jnp.int32)
    offsets = jax.random.permutation(key_offsets, EXPERTS)[:TOPK].astype(jnp.int32)
    hot_columns = (hot_expert + offsets) % EXPERTS
    labels = jnp.arange(EXPERTS, dtype=jnp.int32)
    is_hot = jnp.any(labels[:, None] == hot_columns[None, :], axis=1)
    pool_values = (hot_expert + 1 + jnp.arange((EXPERTS - 1) * CAP, dtype=jnp.int32) // CAP) % EXPERTS

    def one_block(block_key):
        key_pool, key_order, key_labels = jax.random.split(block_key, 3)
        chosen = jax.random.permutation(key_pool, pool_values)[:TOK_DEV - CAP].astype(jnp.int32)
        base_values = jnp.concatenate([jnp.full((CAP,), hot_expert, jnp.int32), chosen])
        base_values = jax.random.permutation(key_order, base_values)
        shifted = (base_values[:, None] + offsets[None, :]) % EXPERTS
        ranks = jax.random.permutation(key_labels, EXPERTS).astype(jnp.int32)
        first_order = jnp.argsort(jnp.where(is_hot, EXPERTS + labels, labels), stable=True)
        second_order = jnp.argsort(jnp.where(is_hot, EXPERTS + labels, ranks), stable=True)
        relabel = jnp.zeros((EXPERTS,), jnp.int32).at[first_order].set(second_order.astype(jnp.int32))
        return relabel[shifted]
    block_keys = jax.random.split(key_blocks, TOKENS // TOK_DEV)
    return jax.vmap(one_block)(block_keys).reshape(TOKENS, TOPK).astype(jnp.int32)


def draw_positives(key, part):
    pair_key = jax.random.fold_in(key, 202)
    order = jax.random.permutation(pair_key, SEQS).astype(jnp.int32)
    first_members = order[0::2]
    second_members = order[1::2]
    partner = jnp.zeros((SEQS,), jnp.int32)
    partner = partner.at[first_members].set(second_members)
    partner = partner.at[second_members].set(first_members)
    return partner


def block_scale(rng, dims, cuts, smallest, largest):
    factor_of, own = 1.0, jax.random.fold_in(rng, 6)
    for dim, blocks in cuts:
        steps = jnp.exp(jax.random.uniform(jax.random.fold_in(own, dim), (blocks,), jnp.float32, smallest / len(cuts), largest / len(cuts)))
        factor_of = factor_of * jnp.repeat(steps, dims[dim] // blocks).reshape([-1 if axis == dim else 1 for axis in range(len(dims))])
    return factor_of


def centred(key, extent, deviation, reach, cuts=(), kind=jnp.bfloat16):
    level = block_scale(key, extent, cuts, -0.22, 0.18) if cuts else 1.0
    values = jax.random.normal(key, extent, jnp.float32) * deviation * level
    return jnp.minimum(jnp.maximum(values, -reach), reach).astype(kind)


def setup_inputs(seed: int = 0) -> dict:
    splits = jax.random.split(jax.random.key(seed), 7)
    return {
        "tokens": centred(splits[0], (TOKENS, D), 1.0, 6.0, ((0, 32),)),
        "expert_ids": draw_expert_ids(jax.random.fold_in(splits[6], 71), 0),
        "gates": jnp.clip(0.05 + 0.2 * jax.random.uniform(splits[2], (TOKENS, TOPK), jnp.float32) ** block_scale(splits[2], (TOKENS, TOPK), ((0, 32), (1, 8)), -0.2, 0.2), 0.05, 0.25),
        "positives": draw_positives(jax.random.fold_in(splits[6], 71), 0),
        "gate_up": centred(splits[4], (SLICES, D, 2 * HALF), D ** -0.5, 0.125, ((0, 256),)),
        "down": centred(splits[5], (SLICES, HALF, D), FF ** -0.5, 0.21875, ((0, 256),)),
    }


logit_divisor = 0.05
grad_scale = 256.0
epsilon = 1e-06

def row_tables(expert_ids):
    blocks = TOKENS // TOK_DEV
    rows_each = blocks * TOPK * CAP
    grouped = expert_ids.reshape(blocks, TOK_DEV, TOPK)
    onehot = (grouped[..., None] == jnp.arange(EXPERTS, dtype=jnp.int32)).astype(jnp.int32)
    before = jnp.cumsum(onehot, axis=1) - onehot
    position = lax.optimization_barrier(jnp.sum(before * onehot, axis=3))
    block_index = jnp.arange(blocks, dtype=jnp.int32)[:, None, None]
    column = jnp.arange(TOPK, dtype=jnp.int32)[None, None, :]
    target = grouped * rows_each + (block_index * TOPK + column) * CAP + position
    token_index = block_index * TOK_DEV + jnp.arange(TOK_DEV, dtype=jnp.int32)[None, :, None]
    token_index = jnp.broadcast_to(token_index, (blocks, TOK_DEV, TOPK))
    table = jnp.full((EXPERTS * rows_each,), TOKENS, jnp.int32)
    table = table.at[target.reshape(-1)].set(token_index.reshape(-1))
    return table.reshape(EXPERTS, rows_each)

def expert_half(expert_rows, weight_in):
    projected = jnp.dot(expert_rows, weight_in, preferred_element_type=jnp.float32)
    gate_part = projected[:, :HALF]
    up_part = projected[:, HALF:]
    sigmoid_gate = jax.nn.sigmoid(gate_part)
    activated = gate_part * sigmoid_gate
    hidden = (activated * up_part).astype(jnp.bfloat16)
    return (gate_part, up_part, sigmoid_gate, activated, hidden)

def reference(tokens, expert_ids, gates, positives, gate_up, down):
    table = row_tables(expert_ids)
    rows_each = table.shape[1]
    column_of_row = jnp.arange(rows_each, dtype=jnp.int32) // CAP % TOPK
    tokens_padded = jnp.concatenate([tokens, jnp.zeros((1, D), tokens.dtype)], axis=0)
    gates_padded = jnp.concatenate([gates, jnp.zeros((1, TOPK), gates.dtype)], axis=0)
    weights_in = gate_up.reshape(EXPERTS, 2, D, 2 * HALF)
    weights_out = down.reshape(EXPERTS, 2, HALF, D)

    def forward_step(accumulated, item_parts):
        entries, pair_in, pair_out = item_parts
        expert_rows = tokens_padded[entries]
        route_total = jnp.zeros((rows_each, D), jnp.float32)
        for half_index in range(2):
            hidden = expert_half(expert_rows, pair_in[half_index])[4]
            half_out = jnp.dot(hidden, pair_out[half_index], preferred_element_type=jnp.float32).astype(jnp.bfloat16)
            route_total = route_total + lax.optimization_barrier(half_out).astype(jnp.float32)
        weight = gates_padded[entries, column_of_row]
        return (accumulated.at[entries].add(weight[:, None] * route_total), None)
    accumulated, _ = lax.scan(forward_step, jnp.zeros((TOKENS + 1, D), jnp.float32), (table, weights_in, weights_out))
    layer_out = (tokens.astype(jnp.float32) + accumulated[:TOKENS]).astype(jnp.bfloat16)
    last_rows = layer_out[LENGTH - 1::LENGTH]
    last_values = last_rows.astype(jnp.float32)
    embedding_lengths = jnp.sqrt(lax.optimization_barrier(jnp.sum(last_values * last_values, axis=1)) + epsilon)
    unit_length_embeddings = last_values / embedding_lengths[:, None]
    pairwise_dots = jnp.dot(last_rows, last_rows.T, preferred_element_type=jnp.float32)
    cosine_logits = pairwise_dots / (embedding_lengths[:, None] * embedding_lengths[None, :]) / logit_divisor
    seq_index = jnp.arange(SEQS, dtype=jnp.int32)
    keep_mask = seq_index[:, None] != seq_index[None, :]
    exp_scores = jnp.where(keep_mask, jnp.exp(cosine_logits), 0.0)
    probabilities = exp_scores / lax.optimization_barrier(jnp.sum(exp_scores, axis=1, keepdims=True))
    target = (seq_index[None, :] == positives[:, None]).astype(jnp.float32)
    objective_multiplier = grad_scale * (probabilities - target)
    slope_wrt_unit_embedding = (jnp.dot(objective_multiplier, unit_length_embeddings, precision=lax.Precision.HIGHEST, preferred_element_type=jnp.float32) + jnp.dot(objective_multiplier.T, unit_length_embeddings, precision=lax.Precision.HIGHEST, preferred_element_type=jnp.float32)) / logit_divisor
    projection = lax.optimization_barrier(jnp.sum(unit_length_embeddings * slope_wrt_unit_embedding, axis=1, keepdims=True))
    grad_last = (slope_wrt_unit_embedding - unit_length_embeddings * projection) / embedding_lengths[:, None]
    grad_padded = jnp.concatenate([grad_last, jnp.zeros((1, D), jnp.float32)], axis=0)

    def backward_step(item_parts):
        entries, pair_in, pair_out = item_parts
        expert_rows = tokens_padded[entries]
        live_rows = (entries < TOKENS) & (entries % LENGTH == LENGTH - 1)
        seq_of_row = jnp.where(live_rows, entries // LENGTH, SEQS).astype(jnp.int32)
        weight = gates_padded[entries, column_of_row]
        route_grad = (weight[:, None] * grad_padded[seq_of_row]).astype(jnp.bfloat16)
        grads_in = []
        grads_out = []
        for half_index in range(2):
            gate_part, up_part, sigmoid_gate, activated, hidden = expert_half(expert_rows, pair_in[half_index])
            grad_hidden = jnp.dot(route_grad, pair_out[half_index].T, preferred_element_type=jnp.float32)
            grads_out.append(jnp.dot(hidden.T, route_grad, preferred_element_type=jnp.float32).astype(jnp.bfloat16))
            gate_slope = sigmoid_gate * (1.0 + gate_part * (1.0 - sigmoid_gate))
            grad_projected = jnp.concatenate([grad_hidden * up_part * gate_slope, grad_hidden * activated], axis=1).astype(jnp.bfloat16)
            grads_in.append(jnp.dot(expert_rows.T, grad_projected, preferred_element_type=jnp.float32).astype(jnp.bfloat16))
        return (jnp.stack(grads_in), jnp.stack(grads_out))
    grads_in, grads_out = lax.map(backward_step, (table, weights_in, weights_out))
    return (layer_out, grads_in.reshape(SLICES, D, 2 * HALF), grads_out.reshape(SLICES, HALF, D))
```

```python
import functools

import jax
import jax.numpy as jnp
from jax import lax
from jax.experimental import pallas as pl
from jax.experimental.pallas import tpu as pltpu
from jax.sharding import PartitionSpec as P

logit_divisor = 0.05
grad_scale = 256.0
epsilon = 1e-06

MESH = pl.DeviceIdType.MESH
NZ, NY, NX, NC = 8, 4, 4, 2
NQ = NY * NX
SLOTS = 32


def layer_kernel(
    tok_hbm, meta_ref, gu_hbm, dn_hbm,
    out_hbm, last_ref, xlast_ref, ml_ref,
    zbuf, mb, mt, rk, gw, tri, sbuf, xm, gu, dn, hid, ys, yo, yr, rs, rbuf, pacc, prec, psend,
    outb, ly, lz, lx, xly, xlz, xlx, mly,
    loc_sem, own_sem, mb_send, mb_recv, mc_send, mc_recv, zs_sem, zr_sem, ms_sem, mr_sem,
    xs_sem, xr_sem, xf_send, xf_recv, ys_send, ys_recv, rs_sem, rr_sem, rown_sem, ps_sem, pr_sem,
    ob_send, ob_recv, oc_send, oc_recv,
    l_send, l_recv, xl_send, xl_recv, mls_sem, mlr_sem,
):
    dp = lax.axis_index("dp")
    ex = lax.axis_index("expert")
    z, y, x, c = dp // NY, dp % NY, ex // NC, ex % NC
    q_me = y * NX + x
    tok, ds = zbuf.shape[1], zbuf.shape[2]
    rows = NY * SLOTS
    core = (dp, x * NC + (1 - c))

    def at(zz, yy, xx):
        return (zz * NY + yy, xx * NC + c)

    def z_line(r):
        return at((z + r) % NZ, y, x)

    def y_line(r):
        return at(z, (y + r) % NY, x)

    def x_line(r):
        return at(z, y, (x + r) % NX)

    def plane(r):
        q = (q_me + r) % NQ
        return q, at(z, q // NX, q % NX)

    def remote(src, dst, send, recv, device):
        return pltpu.make_async_remote_copy(
            src_ref=src, dst_ref=dst, send_sem=send, recv_sem=recv,
            device_id=device, device_id_type=MESH,
        )

    def drain(ref, sem):
        pltpu.make_async_copy(ref, ref, sem).wait()

    col_me = pl.multiple_of(ex * ds, ds)
    tok_load = pltpu.make_async_copy(tok_hbm.at[:, pl.ds(col_me, ds)], zbuf.at[0], loc_sem.at[0])
    tok_load.start()
    half = hid.shape[1]
    nch = gu.shape[0]
    ch = half // nch
    loads = []
    for n in range(nch):
        for part in range(2):
            loads.append(pltpu.make_async_copy(
                gu_hbm.at[:, pl.ds(part * half + n * ch, ch)],
                gu.at[n, :, pl.ds(part * ch, ch)], loc_sem.at[1 + 2 * n + part]))
    for j in range(NX * NC):
        loads.append(pltpu.make_async_copy(
            dn_hbm.at[:, pl.ds(j * ds, ds)], dn.at[j], loc_sem.at[1 + 2 * nch + j]))
    for load in loads:
        load.start()

    barrier = pltpu.get_barrier_semaphore()

    @pl.loop(1, NZ)
    def _(r):
        pl.semaphore_signal(barrier, inc=1, device_id=z_line(r), device_id_type=MESH)

    @pl.loop(1, NQ)
    def _(r):
        pl.semaphore_signal(barrier, inc=1, device_id=plane(r)[1], device_id_type=MESH)

    pl.semaphore_signal(barrier, inc=1, device_id=core, device_id_type=MESH)
    mb[c, x] = meta_ref[...]
    ti = lax.broadcasted_iota(jnp.int32, (tok, tok), 0)
    tj = lax.broadcasted_iota(jnp.int32, (tok, tok), 1)
    tri[...] = jnp.where(ti < tj, 1.0, 0.0).astype(jnp.bfloat16)
    pl.semaphore_wait(barrier, NZ + NQ - 1)

    for r in range(1, NX):
        remote(mb.at[c, x], mb.at[c, x], mb_send.at[r - 1], mb_recv.at[r - 1], x_line(r)).start()

    up, down = z_line(1), z_line(NZ - 1)
    tok_load.wait()
    remote(zbuf.at[0], zbuf.at[1], zs_sem.at[6], zr_sem.at[1], down).start()
    remote(zbuf.at[0], zbuf.at[2], zs_sem.at[0], zr_sem.at[2], up).start()

    per = 4
    length = tok // per
    lrow = lax.broadcasted_iota(jnp.int32, (NY * per, tok), 0)
    ltok = lax.broadcasted_iota(jnp.int32, (NY * per, tok), 1)
    last_sel = jnp.where(
        (ltok % length == length - 1) & (lrow == y * per + ltok // length), 1.0, 0.0
    ).astype(jnp.bfloat16)

    def l_y_start(block, buf, send, recv):
        picked = jnp.dot(last_sel, block, preferred_element_type=jnp.float32)
        buf[y] = picked.astype(jnp.bfloat16)
        for r in range(1, NY):
            remote(buf.at[y], buf.at[y], send.at[r - 1], recv.at[r - 1], y_line(r)).start()

    def l_z_start(ybuf, buf, send, recv):
        for r in range(1, NY):
            drain(ybuf.at[0], recv.at[r - 1])
        total = ybuf[0].astype(jnp.float32)
        for r in range(1, NY):
            total += ybuf[r].astype(jnp.float32)
        buf[z] = total.astype(jnp.bfloat16)
        for r in range(1, NZ):
            remote(buf.at[z], buf.at[z], send.at[2 + r], recv.at[2 + r], z_line(r)).start()

    def l_x_start(zb, buf, send, recv):
        for r in range(1, NZ):
            drain(zb.at[0], recv.at[2 + r])
        buf[c, x] = zb[...].reshape(NZ * NY * per, ds)
        for r in range(1, NX):
            remote(buf.at[c, x], buf.at[c, x], send.at[9 + r], recv.at[9 + r], x_line(r)).start()

    def l_c_start(buf, send, recv):
        for r in range(1, NX):
            drain(buf.at[0, 0], recv.at[9 + r])
        remote(buf.at[c], buf.at[c], send.at[13], recv.at[13], core).start()

    def l_finish(ybuf, zb, buf, out, send, recv):
        drain(buf.at[0], recv.at[13])
        out[...] = buf[...].reshape(out.shape)
        for r in range(1, NY):
            drain(ybuf.at[0], send.at[r - 1])
        for r in range(1, NZ):
            drain(zb.at[0], send.at[2 + r])
        for r in range(1, NX):
            drain(buf.at[0, 0], send.at[9 + r])
        drain(buf.at[0], send.at[13])

    l_y_start(zbuf[0], xly, xl_send, xl_recv)

    for r in range(1, NX):
        drain(mb.at[0, 0], mb_recv.at[r - 1])
    remote(mb.at[c], mb.at[c], mc_send, mc_recv, core).start()
    drain(mb.at[0], mc_recv)
    for part in range(2):
        for side in range(2):
            for cc in range(NC):
                mt[0, part * 8 + cc * NX:part * 8 + (cc + 1) * NX, side * 128:(side + 1) * 128] = (
                    mb[cc, :, 2 * part + side, :])
    for side in range(2):
        mt[0, 16:24, side * 128:(side + 1) * 128] = jnp.broadcast_to(
            mb[0, 0, 4 + side:5 + side, :], (8, 128))
    remote(mt.at[0], mt.at[1], ms_sem.at[6], mr_sem.at[1], down).start()
    remote(mt.at[0], mt.at[2], ms_sem.at[0], mr_sem.at[2], up).start()

    slot_iota = lax.broadcasted_iota(jnp.int32, (SLOTS, tok), 0).astype(jnp.float32)

    def gather_block(i):
        ids = mt[i, 0:8, :]
        gate = mt[i, 8:16, :]
        hits, weights = [], []
        for q in range(NQ):
            hit = ids == (z * NQ + q).astype(jnp.float32)
            hits.append(jnp.sum(jnp.where(hit, 1.0, 0.0), axis=0, keepdims=True))
            weights.append(jnp.sum(jnp.where(hit, gate, 0.0), axis=0, keepdims=True))
        hit = jnp.concatenate(hits, axis=0)
        rank = jnp.dot(hit.astype(jnp.bfloat16), tri[...], preferred_element_type=jnp.float32)
        ranked = jnp.where(hit > 0.0, rank, -1.0)
        rk[i] = ranked
        gw[i] = jnp.concatenate(weights, axis=0)
        picks = jnp.concatenate(
            [jnp.where(slot_iota == ranked[q:q + 1, :], 1.0, 0.0) for q in range(NQ)], axis=0
        ).astype(jnp.bfloat16)
        got = jnp.dot(picks, zbuf[i], preferred_element_type=jnp.float32)
        sbuf[i] = got.astype(jnp.bfloat16).reshape(NQ, SLOTS, ds)

        def place():
            return xm.at[i, pl.ds(pl.multiple_of(y * SLOTS, SLOTS), SLOTS), pl.ds(col_dst, ds)]

        col_dst = pl.multiple_of((x * NC + c) * ds, ds)

        @pl.loop(1, NQ)
        def _(r):
            q, device = plane(r)
            remote(sbuf.at[i, q], place(), xs_sem.at[i], xr_sem.at[i], device).start()

        pltpu.make_async_copy(sbuf.at[i, q_me], place(), own_sem.at[i]).start()

    gather_block(0)

    @pl.loop(1, NZ)
    def _(i):
        drain(zbuf.at[0], zr_sem.at[i])
        drain(mt.at[0], mr_sem.at[i])

        @pl.when(i <= 5)
        def _():
            device = at((z + 1 - 2 * (i % 2) + NZ) % NZ, y, x)
            remote(zbuf.at[i], zbuf.at[i + 2], zs_sem.at[i], zr_sem.at[i + 2], device).start()
            remote(mt.at[i], mt.at[i + 2], ms_sem.at[i], mr_sem.at[i + 2], device).start()

        gather_block(i)

        @pl.when(i == 2)
        def _():
            l_z_start(xly, xlz, xl_send, xl_recv)

        @pl.when(i == 5)
        def _():
            l_x_start(xlz, xlx, xl_send, xl_recv)

    l_c_start(xlx, xl_send, xl_recv)

    total = jnp.zeros((24, NZ * NY * per), jnp.float32)
    st = lax.broadcasted_iota(jnp.int32, (tok, NZ * NY * per), 0)
    sc = lax.broadcasted_iota(jnp.int32, (tok, NZ * NY * per), 1)
    for i in range(NZ):
        zi = (z + ((i + 1) // 2) * (2 * (i % 2) - 1) + NZ) % NZ
        sel = jnp.where(
            (st % length == length - 1) & (sc == (zi * NY + y) * per + st // length), 1.0, 0.0)
        total += jnp.dot(mt[i], sel, precision=lax.Precision.HIGHEST,
                         preferred_element_type=jnp.float32)
    mly[y] = total
    for r in range(1, NY):
        remote(mly.at[y], mly.at[y], mls_sem.at[r - 1], mlr_sem.at[r - 1], y_line(r)).start()

    def forward(i):
        drain(sbuf.at[i, pl.ds(0, NQ - 1)], xr_sem.at[i])
        drain(sbuf.at[0, 0], own_sem.at[i])
        for xx in range(NX):
            cols = pl.ds(pl.multiple_of((xx * NC + c) * ds, ds), ds)
            remote(xm.at[i, :, cols], xm.at[i, :, cols], xf_send.at[i], xf_recv.at[i], core).start()

    for load in loads:
        load.wait()
    forward(0)
    forward(1)

    @pl.loop(0, NZ // 2)
    def _(p):
        @pl.when(p < NZ // 2 - 1)
        def _():
            forward(2 * p + 2)
            forward(2 * p + 3)

        for b in range(2):
            drain(xm.at[0, :, pl.ds(0, NX * ds)], xf_recv.at[2 * p + b])
        xrows = xm[pl.ds(2 * p, 2)].reshape(2 * rows, NX * NC * ds)
        for n in range(nch):
            pr = jnp.dot(xrows, gu[n], preferred_element_type=jnp.float32)
            g, u = pr[:, :ch], pr[:, ch:]
            hid[:, n * ch:(n + 1) * ch] = (g * jax.nn.sigmoid(g) * u).astype(jnp.bfloat16)
        hv = hid[...]
        for xx in range(NX):
            o = jnp.dot(hv, dn[xx * NC + 1 - c], preferred_element_type=jnp.float32)
            o = o.astype(jnp.bfloat16)
            ys[2 * p, xx] = o[:rows]
            ys[2 * p + 1, xx] = o[rows:]
        for b in range(2):
            remote(ys.at[2 * p + b], yr.at[2 * p + b], ys_send.at[2 * p + b],
                   ys_recv.at[2 * p + b], core).start()
        for xx in range(NX):
            o = jnp.dot(hv, dn[xx * NC + c], preferred_element_type=jnp.float32)
            o = o.astype(jnp.bfloat16)
            yo[2 * p, xx] = o[:rows]
            yo[2 * p + 1, xx] = o[rows:]

    @pl.loop(0, NZ)
    def _(n):
        i = NZ - 1 - n
        drain(ys.at[0], ys_recv.at[i])
        rs[i] = (yo[i].astype(jnp.float32) + yr[i].astype(jnp.float32)).astype(jnp.bfloat16)

        def piece(q):
            return rs.at[i, q % NX, pl.ds(pl.multiple_of((q // NX) * SLOTS, SLOTS), SLOTS)]

        @pl.loop(1, NQ)
        def _(r):
            q, device = plane(r)
            remote(piece(q), rbuf.at[i, q_me], rs_sem.at[i], rr_sem.at[i], device).start()

        pltpu.make_async_copy(piece(q_me), rbuf.at[i, q_me], rown_sem.at[i]).start()

    def combine(i):
        drain(sbuf.at[i, pl.ds(0, NQ - 1)], rr_sem.at[i])
        drain(sbuf.at[0, 0], rown_sem.at[i])
        ranked, w = rk[i], gw[i]
        spread = jnp.concatenate(
            [jnp.where(slot_iota == ranked[q:q + 1, :], w[q:q + 1, :], 0.0) for q in range(NQ)],
            axis=0,
        ).astype(jnp.bfloat16)
        return lax.dot_general(
            spread, rbuf[i].reshape(NQ * SLOTS, ds), (((0,), (0,)), ((), ())),
            preferred_element_type=jnp.float32)

    @pl.loop(0, NZ - 1)
    def _(n):
        i = NZ - 1 - n
        part = combine(i)
        pacc[i] = part

        @pl.when(i <= 5)
        def _():
            drain(prec.at[0], pr_sem.at[i])
            pacc[i] += prec[i].astype(jnp.float32)

        prec_out = pacc[i].astype(jnp.bfloat16)
        psend[i] = prec_out
        slot = (i + 5) % 7
        device = at((z - 1 + 2 * (i % 2) + NZ) % NZ, y, x)
        remote(psend.at[i], prec.at[slot], ps_sem.at[i], pr_sem.at[slot], device).start()

    part = combine(0)
    drain(prec.at[0], pr_sem.at[0])
    drain(prec.at[0], pr_sem.at[6])
    part += prec[0].astype(jnp.float32) + prec[6].astype(jnp.float32)
    block = (zbuf[0].astype(jnp.float32) + part).astype(jnp.bfloat16)
    outb[c, x] = block
    l_y_start(block, ly, l_send, l_recv)
    for r in range(1, NX):
        remote(outb.at[c, x], outb.at[c, x], ob_send.at[r - 1], ob_recv.at[r - 1], x_line(r)).start()
    l_z_start(ly, lz, l_send, l_recv)
    for r in range(1, NX):
        drain(outb.at[0, 0], ob_recv.at[r - 1])
    remote(outb.at[c], outb.at[c], oc_send, oc_recv, core).start()
    l_x_start(lz, lx, l_send, l_recv)
    l_c_start(lx, l_send, l_recv)

    for r in range(1, NY):
        drain(mly.at[0], mlr_sem.at[r - 1])
    ml_ref[...] = mly[0] + mly[1] + mly[2] + mly[3]
    l_finish(xly, xlz, xlx, xlast_ref, xl_send, xl_recv)

    drain(outb.at[0], oc_recv)
    writes = []
    for cc in range(NC):
        for xx in range(NX):
            j = xx * NC + cc
            writes.append(pltpu.make_async_copy(
                outb.at[cc, xx], out_hbm.at[:, pl.ds(j * ds, ds)], loc_sem.at[1 + j]))
    for write in writes:
        write.start()
    l_finish(ly, lz, lx, last_ref, l_send, l_recv)
    for write in writes:
        write.wait()

    for r in range(1, NX):
        drain(mb.at[0, 0], mb_send.at[r - 1])
        drain(outb.at[0, 0], ob_send.at[r - 1])
    drain(mb.at[0], mc_send)
    drain(outb.at[0], oc_send)
    for r in range(1, NY):
        drain(mly.at[0], mls_sem.at[r - 1])
    for i in range(7):
        drain(zbuf.at[0], zs_sem.at[i])
        drain(mt.at[0], ms_sem.at[i])

    @pl.loop(0, NZ)
    def _(i):
        drain(sbuf.at[0, pl.ds(0, NQ - 1)], xs_sem.at[i])
        drain(sbuf.at[0, pl.ds(0, NQ - 1)], rs_sem.at[i])
        drain(xm.at[0, :, pl.ds(0, NX * ds)], xf_send.at[i])
        drain(ys.at[0], ys_send.at[i])

    @pl.loop(1, NZ)
    def _(i):
        drain(zbuf.at[0], ps_sem.at[i])


def layer_call(tokens, meta, gate_up, down):
    tok, width = tokens.shape
    half = down.shape[0]
    ds = width // (NX * NC)
    rows = NY * SLOTS
    seqs = NZ * NY * 4
    bf, f32 = jnp.bfloat16, jnp.float32
    dma = pltpu.SemaphoreType.DMA
    vm = pltpu.VMEM
    scratch = [
        vm((NZ, tok, ds), bf),
        vm((NC, NX, 8, 128), f32),
        vm((NZ, 24, tok), f32),
        vm((NZ, NQ, tok), f32),
        vm((NZ, NQ, tok), f32),
        vm((tok, tok), bf),
        vm((NZ, NQ, SLOTS, ds), bf),
        vm((NZ, rows, width), bf),
        vm((3, width, 2 * half // 3), bf),
        vm((NX * NC, half, ds), bf),
        vm((2 * rows, half), bf),
        vm((NZ, NX, rows, ds), bf),
        vm((NZ, NX, rows, ds), bf),
        vm((NZ, NX, rows, ds), bf),
        vm((NZ, NX, rows, ds), bf),
        vm((NZ, NQ, SLOTS, ds), bf),
        vm((NZ, tok, ds), f32),
        vm((7, tok, ds), bf),
        vm((NZ, tok, ds), bf),
        vm((NC, NX, tok, ds), bf),
        vm((NY, NY * 4, ds), bf),
        vm((NZ, NY * 4, ds), bf),
        vm((NC, NX, seqs, ds), bf),
        vm((NY, NY * 4, ds), bf),
        vm((NZ, NY * 4, ds), bf),
        vm((NC, NX, seqs, ds), bf),
        vm((NY, 24, seqs), f32),
        dma((16,)), dma((NZ,)), dma((3,)), dma((3,)), dma, dma,
        dma((7,)), dma((NZ,)), dma((7,)), dma((NZ,)),
        dma((NZ,)), dma((NZ,)), dma((NZ,)), dma((NZ,)), dma((NZ,)), dma((NZ,)),
        dma((NZ,)), dma((NZ,)), dma((NZ,)), dma((NZ,)), dma((NZ,)),
        dma((3,)), dma((3,)), dma, dma,
        dma((14,)), dma((14,)), dma((14,)), dma((14,)), dma((3,)), dma((3,)),
    ]
    anyspec = pl.BlockSpec(memory_space=pl.ANY)
    vspec = pl.BlockSpec(memory_space=pltpu.VMEM)
    return pl.pallas_call(
        layer_kernel,
        out_shape=(
            jax.ShapeDtypeStruct((tok, width), bf),
            jax.ShapeDtypeStruct((NC, NX, seqs, ds), bf),
            jax.ShapeDtypeStruct((NC, NX, seqs, ds), bf),
            jax.ShapeDtypeStruct((24, seqs), f32),
        ),
        in_specs=[anyspec, vspec, anyspec, anyspec],
        out_specs=(anyspec, vspec, vspec, vspec),
        scratch_shapes=scratch,
        compiler_params=pltpu.CompilerParams(
            collective_id=0, has_side_effects=True, vmem_limit_bytes=60 * 1024 * 1024),
        name="layer",
    )(tokens, meta, gate_up, down)


def unslice(sliced):
    cores, xs, seqs, ds = sliced.shape
    return sliced.transpose(2, 1, 0, 3).reshape(seqs, cores * xs * ds)


def body(tokens, expert_ids, gates, positives, gate_up, down):
    dp = lax.axis_index("dp")
    ex = lax.axis_index("expert")
    weight_in, weight_out = gate_up[0], down[0]
    half = weight_out.shape[0]
    meta = jnp.concatenate([
        expert_ids.astype(jnp.float32).reshape(2, 128),
        gates.reshape(2, 128),
        jnp.repeat(positives.astype(jnp.float32), tokens.shape[0] // positives.shape[0]).reshape(2, 128),
        jnp.zeros((2, 128), jnp.float32),
    ], axis=0)
    layer_out, last, xlast, ml = layer_call(tokens, meta, weight_in, weight_out)
    last = unslice(last)
    xlast = unslice(xlast)
    seqs = last.shape[0]
    values = last.astype(jnp.float32)
    norms = jnp.sqrt(jnp.sum(values * values, axis=1) + epsilon)
    unit = values / norms[:, None]
    dots = lax.dot_general(last, last, (((1,), (1,)), ((), ())), preferred_element_type=jnp.float32)
    scores = dots / (norms[:, None] * norms[None, :]) / logit_divisor
    index = jnp.arange(seqs, dtype=jnp.int32)
    exps = jnp.where(index[:, None] != index[None, :], jnp.exp(scores), 0.0)
    prob = exps / jnp.sum(exps, axis=1, keepdims=True)
    target = (index[None, :] == ml[16].astype(jnp.int32)[:, None]).astype(jnp.float32)
    coef = grad_scale * (prob - target)
    slope = jnp.dot(
        coef + coef.T, unit, precision=lax.Precision.HIGHEST, preferred_element_type=jnp.float32
    ) / logit_divisor
    proj = jnp.sum(unit * slope, axis=1, keepdims=True)
    grad_last = (slope - unit * proj) / norms[:, None]
    expert = (dp * NX + ex // NC).astype(jnp.float32)
    weight = jnp.sum(jnp.where(ml[:8] == expert, ml[8:16], 0.0), axis=0)
    route_grad = (weight[:, None] * grad_last).astype(jnp.bfloat16)
    projected = jnp.dot(xlast, weight_in, preferred_element_type=jnp.float32)
    gate_part, up_part = projected[:, :half], projected[:, half:]
    sig = jax.nn.sigmoid(gate_part)
    activated = gate_part * sig
    hidden = (activated * up_part).astype(jnp.bfloat16)
    grad_hidden = lax.dot_general(
        route_grad, weight_out, (((1,), (1,)), ((), ())), preferred_element_type=jnp.float32)
    contract = functools.partial(
        lax.dot_general, dimension_numbers=(((0,), (0,)), ((), ())),
        preferred_element_type=jnp.float32)
    grad_down = contract(hidden, route_grad).astype(jnp.bfloat16)
    slope_gate = sig * (1.0 + gate_part * (1.0 - sig))
    grad_projected = jnp.concatenate(
        [grad_hidden * up_part * slope_gate, grad_hidden * activated], axis=1
    ).astype(jnp.bfloat16)
    grad_gate_up = contract(xlast, grad_projected).astype(jnp.bfloat16)
    return layer_out, grad_gate_up[None], grad_down[None]


def solution(mesh):
    return jax.shard_map(
        body,
        mesh=mesh,
        in_specs=(
            P("dp", None),
            P("dp", "expert"),
            P("dp", "expert"),
            P("dp"),
            P(("dp", "expert"), None, None),
            P(("dp", "expert"), None, None),
        ),
        out_specs=(P("dp", None), P(("dp", "expert"), None, None), P(("dp", "expert"), None, None)),
        check_vma=False,
    )
```

```python
import functools

import jax
import jax.numpy as jnp
from jax import lax
from jax.experimental import pallas as pl
from jax.experimental.pallas import tpu as pltpu
from jax.sharding import PartitionSpec as P

logit_divisor = 0.05
grad_scale = 256.0
epsilon = 1e-06

MESH = pl.DeviceIdType.MESH
NZ, NY, NX, NC = 8, 4, 4, 2
NQ = NY * NX
SLOTS = 32


def layer_kernel(
    tok_hbm, ids_ref, gates_ref, pos_ref, gu_hbm, dn_hbm,
    out_hbm, xlast_hbm, hid_hbm, rg_hbm, gp_hbm,
    zbuf, tokc, mb, mo, mt, rk, gw, tri, sbuf, xm, gu, dn, hid, ys, yo, yr, rs, rbuf, prec, psend, pacc, outb,
    xly, mly, xlz, mlz, plast, kls, klo, klr, kz, kzr, ky, kx, lastz, xlast_ref, hid_ref, rg_ref, gp_ref,
    loc_sem, own_sem, mb_send, mb_recv, zs_sem, zr_sem, ms_sem, mr_sem,
    xs_sem, xr_sem, xf_send, xf_recv, ys_send, ys_recv, rs_sem, rr_sem, rown_sem, ps_sem, pr_sem,
    ob_send, ob_recv, oc_send, oc_recv,
    xly_send, xly_recv, mly_send, mly_recv, xlz_send, xlz_recv, mlz_send, mlz_recv,
    xlc_send, xlc_recv, klc_send, klc_recv, kz_send, kz_recv, ky_send, ky_recv, kx_send, kx_recv,
    lz_send, lz_recv, lc_send, lc_recv, out_sem,
):
    dp = lax.axis_index("dp")
    ex = lax.axis_index("expert")
    z, y, x, c = dp // NY, dp % NY, ex // NC, ex % NC
    q_me = y * NX + x
    tok, ds = zbuf.shape[1], zbuf.shape[2]
    rows = NY * SLOTS
    hw = NX * ds
    seqs = plast.shape[0]
    per = seqs // (NZ * NY)
    length = tok // per
    core = (dp, x * NC + (1 - c))
    f32, bf = jnp.float32, jnp.bfloat16

    def at(zz, yy, xx):
        return (zz * NY + yy, xx * NC + c)

    def z_line(r):
        return at((z + r) % NZ, y, x)

    def y_line(r):
        return at(z, (y + r) % NY, x)

    def x_line(r):
        return at(z, y, (x + r) % NX)

    def group(r):
        return (dp, (ex + r) % (NX * NC))

    def plane(r):
        q = (q_me + r) % NQ
        return q, at(z, q // NX, q % NX)

    def plane_of(i):
        return (z + ((i + 1) // 2) * (2 * (i % 2) - 1) + NZ) % NZ

    def remote(src, dst, send, recv, device):
        return pltpu.make_async_remote_copy(
            src_ref=src, dst_ref=dst, send_sem=send, recv_sem=recv,
            device_id=device, device_id_type=MESH,
        )

    def drain(ref, sem):
        pltpu.make_async_copy(ref, ref, sem).wait()

    def signal(device):
        pl.semaphore_signal(barrier, inc=1, device_id=device, device_id_type=MESH)

    half = hid.shape[1]
    nch = gu.shape[0]
    ch = half // nch
    col_me = pl.multiple_of(ex * ds, ds)
    tok_load = pltpu.make_async_copy(tok_hbm.at[:, pl.ds(col_me, ds)], zbuf.at[0], loc_sem.at[0])
    tok_load.start()
    tok_loads = [
        pltpu.make_async_copy(
            tok_hbm.at[:, pl.ds(pl.multiple_of((xx * NC + c) * ds, ds), ds)], tokc.at[xx],
            loc_sem.at[1 + xx])
        for xx in range(NX)
    ]
    for load in tok_loads:
        load.start()
    loads = []
    for n in range(nch):
        for part in range(2):
            loads.append(pltpu.make_async_copy(
                gu_hbm.at[:, pl.ds(part * half + n * ch, ch)],
                gu.at[n, :, pl.ds(part * ch, ch)], loc_sem.at[5 + 2 * n + part]))
    for j in range(NX * NC):
        loads.append(pltpu.make_async_copy(
            dn_hbm.at[:, pl.ds(j * ds, ds)], dn.at[j], loc_sem.at[5 + 2 * nch + j]))

    for load in loads:
        load.start()

    barrier = pltpu.get_barrier_semaphore()

    @pl.loop(1, NZ)
    def _(r):
        signal(z_line(r))

    @pl.loop(1, NQ)
    def _(r):
        signal(plane(r)[1])

    signal(core)
    for r in range(1, NX):
        signal((dp, (x + r) % NX * NC + (1 - c)))

    lane = lax.broadcasted_iota(jnp.int32, (1, 128), 1)
    mb[c, x, 0:2, :] = ids_ref[...].astype(f32)
    mb[c, x, 2:4, :] = gates_ref[...]
    mb[c, x, 4:5, :] = jnp.where(lane < length, pos_ref[0], pos_ref[1]).astype(f32)
    mb[c, x, 5:6, :] = jnp.where(lane < length, pos_ref[2], pos_ref[3]).astype(f32)
    mb[c, x, 6:8, :] = jnp.zeros((2, 128), f32)
    ti = lax.broadcasted_iota(jnp.int32, (tok, tok), 0)
    tj = lax.broadcasted_iota(jnp.int32, (tok, tok), 1)
    tri[...] = jnp.where(ti < tj, 1.0, 0.0).astype(bf)

    lrow = lax.broadcasted_iota(jnp.int32, (NY * per, tok), 0)
    ltok = lax.broadcasted_iota(jnp.int32, (NY * per, tok), 1)
    last_sel = jnp.where(
        (ltok % length == length - 1) & (lrow == y * per + ltok // length), 1.0, 0.0)
    for load in tok_loads:
        load.wait()
    for xx in range(NX):
        xly[y, :, xx * ds:(xx + 1) * ds] = jnp.dot(
            last_sel.astype(bf), tokc[xx], preferred_element_type=f32).astype(bf)
    mly[y] = jnp.zeros((NY * per, 128), f32)
    tok_load.wait()
    pl.semaphore_wait(barrier, NZ + NQ - 1 + NX - 1)

    for r in range(1, NX * NC):
        remote(mb.at[c, x], mb.at[c, x], mb_send.at[r - 1], mb_recv.at[r - 1], group(r)).start()

    up, down = z_line(1), z_line(NZ - 1)

    def ring_own(view, down_view, up_view, send, recv):
        remote(view, down_view, send.at[6], recv.at[1], down).start()
        remote(view, up_view, send.at[0], recv.at[2], up).start()

    def ring_on(i, view, next_view, send, recv):
        device = at((z + 1 - 2 * (i % 2) + NZ) % NZ, y, x)
        remote(view, next_view, send.at[i], recv.at[i + 2], device).start()

    ring_own(zbuf.at[0], zbuf.at[1], zbuf.at[2], zs_sem, zr_sem)
    for r in range(1, NY):
        remote(xly.at[y], xly.at[y], xly_send.at[r - 1], xly_recv.at[r - 1], y_line(r)).start()

    for r in range(1, NX * NC):
        drain(mb.at[0, 0], mb_recv.at[r - 1])
    for side in range(2):
        cols = slice(side * 128, (side + 1) * 128)
        for part in range(2):
            for cc in range(NC):
                mo[part * 8 + cc * NX:part * 8 + (cc + 1) * NX, cols] = mb[cc, :, 2 * part + side, :]
        mo[16:24, cols] = jnp.broadcast_to(mb[0, 0, 4 + side:5 + side, :], (8, 128))
    mt[0] = mo[0:16, :].astype(bf)
    ring_own(mt.at[0], mt.at[1], mt.at[2], ms_sem, mr_sem)

    slot_iota = lax.broadcasted_iota(jnp.int32, (SLOTS, tok), 0).astype(f32)

    def gather_block(i):
        table = mt[i].astype(f32)
        ids, gate = table[0:8], table[8:16]
        hits, weights = [], []
        for q in range(NQ):
            hit = ids == (z * NQ + q).astype(f32)
            hits.append(jnp.sum(jnp.where(hit, 1.0, 0.0), axis=0, keepdims=True))
            weights.append(jnp.sum(jnp.where(hit, gate, 0.0), axis=0, keepdims=True))
        hit = jnp.concatenate(hits, axis=0)
        rank = jnp.dot(hit.astype(bf), tri[...], preferred_element_type=f32)
        ranked = jnp.where(hit > 0.0, rank, -1.0)
        rk[i] = ranked
        gw[i] = jnp.concatenate(weights, axis=0)
        picks = jnp.concatenate(
            [jnp.where(slot_iota == ranked[q:q + 1, :], 1.0, 0.0) for q in range(NQ)], axis=0
        ).astype(bf)
        got = jnp.dot(picks, zbuf[i], preferred_element_type=f32)
        sbuf[i] = got.astype(bf).reshape(NQ, SLOTS, ds)

        def place():
            return xm.at[i, pl.ds(pl.multiple_of(y * SLOTS, SLOTS), SLOTS), pl.ds(col_me, ds)]

        @pl.loop(1, NQ)
        def _(r):
            q, device = plane(r)
            remote(sbuf.at[i, q], place(), xs_sem.at[i], xr_sem.at[i], device).start()

        pltpu.make_async_copy(sbuf.at[i, q_me], place(), own_sem.at[i]).start()

    gather_block(0)

    mly[y, :, 0:24] = lax.dot_general(
        last_sel, mo[...], (((1,), (1,)), ((), ())), precision=lax.Precision.HIGHEST,
        preferred_element_type=f32)
    for r in range(1, NY):
        remote(mly.at[y], mly.at[y], mly_send.at[r - 1], mly_recv.at[r - 1], y_line(r)).start()
    def last_rows_own():
        for r in range(1, NY):
            drain(xly.at[0], xly_recv.at[r - 1])
        total = xly[0].astype(f32)
        for r in range(1, NY):
            total += xly[r].astype(f32)
        xlz[c, z] = total.astype(bf)
        for r in range(1, NY):
            drain(mly.at[0], mly_recv.at[r - 1])
        mlz[z] = mly[0] + mly[1] + mly[2] + mly[3]
        for r in range(1, NZ):
            remote(xlz.at[c, z], xlz.at[c, z], xlz_send.at[r - 1], xlz_recv.at[r - 1],
                   z_line(r)).start()
            remote(mlz.at[z], mlz.at[z], mlz_send.at[r - 1], mlz_recv.at[r - 1], z_line(r)).start()

    def forward(i):
        drain(sbuf.at[0, pl.ds(0, NQ - 1)], xr_sem.at[i])
        drain(sbuf.at[0, 0], own_sem.at[i])
        for xx in range(NX):
            cols = pl.ds(pl.multiple_of((xx * NC + c) * ds, ds), ds)
            remote(xm.at[i, :, cols], xm.at[i, :, cols], xf_send.at[i], xf_recv.at[i], core).start()

    def silu_mul(pr):
        g, u = pr[:, :ch], pr[:, ch:]
        return (g * jax.nn.sigmoid(g) * u).astype(bf)

    def experts(p):
        for b in range(2):
            drain(xm.at[0, :, pl.ds(0, hw)], xf_recv.at[2 * p + b])
        xrows = xm[pl.ds(2 * p, 2)].reshape(2 * rows, NC * hw)
        for n in range(nch):
            hid[:, n * ch:(n + 1) * ch] = silu_mul(
                jnp.dot(xrows, gu[n], preferred_element_type=f32))
        hv = hid[...]
        for xx in range(NX):
            o = jnp.dot(hv, dn[xx * NC + 1 - c], preferred_element_type=f32).astype(bf)
            ys[2 * p, xx] = o[:rows]
            ys[2 * p + 1, xx] = o[rows:]
        for b in range(2):
            remote(ys.at[2 * p + b], yr.at[2 * p + b], ys_send.at[2 * p + b],
                   ys_recv.at[2 * p + b], core).start()
        for xx in range(NX):
            o = jnp.dot(hv, dn[xx * NC + c], preferred_element_type=f32).astype(bf)
            yo[2 * p, xx] = o[:rows]
            yo[2 * p + 1, xx] = o[rows:]

    def all_columns(buf, j):
        part = buf[j % NC, :, :, (j // NC) * ds:(j // NC + 1) * ds]
        return part.reshape(seqs, ds)

    def experts_last():
        drain(xlz.at[0], xlc_recv)
        xrows = jnp.concatenate([all_columns(xlz, j) for j in range(NX * NC)], axis=1)
        for n in range(nch):
            pr = jnp.dot(xrows, gu[n], preferred_element_type=f32)
            plast[:, 2 * n * ch:2 * (n + 1) * ch] = pr
            hid[:seqs, n * ch:(n + 1) * ch] = silu_mul(pr)
        hv = hid[:seqs]
        hid_ref[...] = hv.astype(f32).T.astype(bf)
        for xx in range(NX):
            o = jnp.dot(hv, dn[xx * NC + 1 - c], preferred_element_type=f32).astype(bf)
            kls[:, :, xx * ds:(xx + 1) * ds] = o.reshape(NZ, NY * per, ds)
        remote(kls, klr, klc_send, klc_recv, core).start()
        for xx in range(NX):
            o = jnp.dot(hv, dn[xx * NC + c], preferred_element_type=f32).astype(bf)
            klo[:, :, xx * ds:(xx + 1) * ds] = o.reshape(NZ, NY * per, ds)

    lanes = lax.broadcasted_iota(jnp.int32, (seqs, 128), 1)

    def last_weight():
        m = mlz[...].reshape(seqs, 128)
        mine = (m == (dp * NX + x).astype(f32)) & (lanes < 8)
        return jnp.sum(jnp.where(mine, pltpu.roll(m, 120, 1), 0.0), axis=1, keepdims=True)

    def last_to_planes():
        drain(klr, klc_recv)
        both = klo[...].astype(f32) + klr[...].astype(f32)
        kz[...] = (both.reshape(seqs, hw) * last_weight()).astype(bf).reshape(NZ, NY * per, hw)
        for r in range(1, NZ):
            remote(kz.at[(z + r) % NZ], kzr.at[z], kz_send.at[r - 1], kz_recv.at[r - 1],
                   z_line(r)).start()

    def last_to_y():
        for r in range(1, NZ):
            drain(kz.at[0], kz_recv.at[r - 1])
        total = kz[z].astype(f32)
        for r in range(1, NZ):
            total += kzr[(z + r) % NZ].astype(f32)
        ky[y] = total.astype(bf)
        for r in range(1, NY):
            remote(ky.at[y], ky.at[y], ky_send.at[r - 1], ky_recv.at[r - 1], y_line(r)).start()

    def last_to_x():
        for r in range(1, NY):
            drain(ky.at[0], ky_recv.at[r - 1])
        total = ky[0].astype(f32)
        for r in range(1, NY):
            total += ky[r].astype(f32)
        kx[x] = total.astype(bf)
        for r in range(1, NX):
            remote(kx.at[x], kx.at[x], kx_send.at[r - 1], kx_recv.at[r - 1], x_line(r)).start()

    def last_to_all():
        for r in range(1, NX):
            drain(kx.at[0], kx_recv.at[r - 1])
        total = kx[0].astype(f32)
        for r in range(1, NX):
            total += kx[r].astype(f32)
        lastz[c, z] = (xlz[c, z].astype(f32) + total).astype(bf)
        for r in range(1, NZ):
            remote(lastz.at[c, z], lastz.at[c, z], lz_send.at[r - 1], lz_recv.at[r - 1],
                   z_line(r)).start()

    def last_to_core():
        for r in range(1, NZ):
            drain(kz.at[0], lz_recv.at[r - 1])
        remote(lastz.at[c], lastz.at[c], lc_send, lc_recv, core).start()

    def loss_and_rows():
        drain(lastz.at[0], lc_recv)
        dots = jnp.zeros((seqs, seqs), f32)
        for cc in range(NC):
            part = lastz[cc].reshape(seqs, hw)
            dots += lax.dot_general(
                part, part, (((1,), (1,)), ((), ())), preferred_element_type=f32)
        ri = lax.broadcasted_iota(jnp.int32, (seqs, seqs), 0)
        cj = lax.broadcasted_iota(jnp.int32, (seqs, seqs), 1)
        eye = ri == cj
        squares = jnp.where(eye, dots, 0.0)
        n_col = jnp.sqrt(jnp.sum(squares, axis=1, keepdims=True) + epsilon)
        n_row = jnp.sqrt(jnp.sum(squares, axis=0, keepdims=True) + epsilon)
        scores = dots / (n_col * n_row) / logit_divisor
        exps = jnp.where(eye, 0.0, jnp.exp(scores))
        prob = exps / jnp.sum(exps, axis=1, keepdims=True)
        m = mlz[...].reshape(seqs, 128)
        positive = jnp.sum(jnp.where(lanes == 16, m, 0.0), axis=1, keepdims=True)
        coef = grad_scale * (prob - jnp.where(cj.astype(f32) == positive, 1.0, 0.0))
        both = coef + coef.T
        proj = jnp.sum(both * scores, axis=1, keepdims=True)
        mat = (both / (n_row * logit_divisor) - jnp.where(eye, proj / n_col, 0.0)) / n_col
        mat = mat * last_weight()
        first = mat.astype(bf)
        rest = mat - first.astype(f32)
        second = rest.astype(bf)
        third = (rest - second.astype(f32)).astype(bf)
        grad_hidden = jnp.zeros((seqs, half), f32)
        for j in range(NX * NC):
            lj = all_columns(lastz, j)
            g = jnp.dot(first, lj, preferred_element_type=f32)
            g += jnp.dot(second, lj, preferred_element_type=f32)
            g += jnp.dot(third, lj, preferred_element_type=f32)
            g = g.astype(bf)
            rg_ref[:, j * ds:(j + 1) * ds] = g
            xlast_ref[j * ds:(j + 1) * ds, :] = all_columns(xlz, j).astype(f32).T.astype(bf)
            grad_hidden += lax.dot_general(
                g, dn[j], (((1,), (1,)), ((), ())), preferred_element_type=f32)
        for n in range(nch):
            gate_part = plast[:, 2 * n * ch:(2 * n + 1) * ch]
            up_part = plast[:, (2 * n + 1) * ch:2 * (n + 1) * ch]
            gh = grad_hidden[:, n * ch:(n + 1) * ch]
            sig = jax.nn.sigmoid(gate_part)
            gp_ref[:, n * ch:(n + 1) * ch] = (
                gh * up_part * (sig * (1.0 + gate_part * (1.0 - sig)))).astype(bf)
            gp_ref[:, half + n * ch:half + (n + 1) * ch] = (gh * (gate_part * sig)).astype(bf)

    def swap_last_rows():
        for r in range(NZ - 1):
            drain(xlz.at[0, 0], xlz_recv.at[r])
            drain(mlz.at[0], mlz_recv.at[r])
        remote(xlz.at[c], xlz.at[c], xlc_send, xlc_recv, core).start()

    def send_back(i):
        drain(ys.at[0], ys_recv.at[i])
        rs[i] = (yo[i].astype(f32) + yr[i].astype(f32)).astype(bf)

        def piece(q):
            return rs.at[i, q % NX, pl.ds(pl.multiple_of((q // NX) * SLOTS, SLOTS), SLOTS)]

        @pl.loop(1, NQ)
        def _(r):
            q, device = plane(r)
            remote(piece(q), rbuf.at[i, q_me], rs_sem.at[i], rr_sem.at[i], device).start()

        pltpu.make_async_copy(piece(q_me), rbuf.at[i, q_me], rown_sem.at[i]).start()

    @pl.loop(1, 11)
    def _(i):
        @pl.when((i == 7) | (i == 9) | (i == 10))
        def _():
            experts((i - 7) // 2 + (i // 10))

        @pl.when(i < NZ)
        def _():
            drain(zbuf.at[0], zr_sem.at[i])
            drain(mt.at[0], mr_sem.at[i])

            @pl.when(i <= 5)
            def _():
                ring_on(i, zbuf.at[i], zbuf.at[i + 2], zs_sem, zr_sem)
                ring_on(i, mt.at[i], mt.at[i + 2], ms_sem, mr_sem)

            gather_block(i)

        @pl.when(i >= 5)
        def _():
            forward(i - 5 + (i + 1) // 8 + i // 10)

        @pl.when((i == 6) | (i == 9))
        def _():
            forward(2 + 4 * (i // 9))

        @pl.when(i == 5)
        def _():
            for load in loads:
                load.wait()

        @pl.when(i == 6)
        def _():
            last_rows_own()

        @pl.when(i == 9)
        def _():
            swap_last_rows()

    send_back(5)
    send_back(4)
    experts_last()
    experts(NZ // 2 - 1)
    last_to_planes()

    def arrived(i):
        drain(sbuf.at[0, pl.ds(0, NQ - 1)], rr_sem.at[i])
        drain(sbuf.at[0, 0], rown_sem.at[i])

    def combine(i):
        ranked, w = rk[i], gw[i]
        spread = jnp.concatenate(
            [jnp.where(slot_iota == ranked[q:q + 1, :], w[q:q + 1, :], 0.0) for q in range(NQ)],
            axis=0,
        ).astype(bf)
        return lax.dot_general(
            spread, rbuf[i].reshape(NQ * SLOTS, ds), (((0,), (0,)), ((), ())),
            preferred_element_type=f32)


    row_copies = [
        pltpu.make_async_copy(src, dst, out_sem.at[8 + n]) for n, (src, dst) in enumerate((
            (xlast_ref, xlast_hbm), (hid_ref, hid_hbm), (rg_ref, rg_hbm), (gp_ref, gp_hbm)))]

    def drained_early():
        for r in range(NX * NC - 1):
            drain(mb.at[0, 0], mb_send.at[r])
        for r in range(NY - 1):
            drain(xly.at[0], xly_send.at[r])
            drain(mly.at[0], mly_send.at[r])
        for r in range(NZ - 1):
            drain(zbuf.at[0], zs_sem.at[r])
            drain(mt.at[0], ms_sem.at[r])
            drain(xlz.at[0, 0], xlz_send.at[r])
            drain(mlz.at[0], mlz_send.at[r])
        drain(xlz.at[0], xlc_send)
        drain(kls, klc_send)
        for n in range(NZ):
            drain(sbuf.at[0, pl.ds(0, NQ - 1)], xs_sem.at[n])
            drain(xm.at[0, :, pl.ds(0, hw)], xf_send.at[n])

    def order(n):
        return NZ - 1 - n + (1 - n // 4) * (4 * (n // 2 % 2) - 2)

    def sum_on(i):
        slot = (i + 5) % 7
        device = at((z - 1 + 2 * (i % 2) + NZ) % NZ, y, x)
        remote(psend.at[i], prec.at[slot], ps_sem.at[i], pr_sem.at[slot], device).start()

    def add_on(i):
        drain(prec.at[0], pr_sem.at[i])
        psend[i] = (pacc[i - 4] + prec[i].astype(f32)).astype(bf)
        sum_on(i)

    @pl.loop(0, NZ - 1)
    def _(n):
        i = order(n)
        arrived(i)

        @pl.when(n <= NZ - 3)
        def _():
            send_back(order(n + 2))

        part = combine(i)

        @pl.when(n < 2)
        def _():
            pacc[1 - n] = part

        @pl.when((n >= 2) & (n < 4))
        def _():
            psend[i] = part.astype(bf)
            sum_on(i)

        @pl.when(n == 3)
        def _():
            add_on(5)

        @pl.when(n == 4)
        def _():
            add_on(4)

        @pl.when(n >= 4)
        def _():
            drain(prec.at[0], pr_sem.at[i])
            psend[i] = (part + prec[i].astype(f32)).astype(bf)
            sum_on(i)

        @pl.when(n == 0)
        def _():
            drained_early()

        @pl.when(n == 2)
        def _():
            last_to_y()

        @pl.when(n == 4)
        def _():
            last_to_x()

        @pl.when(n == 6)
        def _():
            last_to_all()

    arrived(0)
    part = combine(0)
    drain(prec.at[0], pr_sem.at[0])
    drain(prec.at[0], pr_sem.at[6])
    part += prec[0].astype(f32) + prec[6].astype(f32)
    outb[c, x] = (zbuf[0].astype(f32) + part).astype(bf)
    remote(outb.at[c, x], outb.at[c, x], oc_send.at[0], oc_recv.at[0], core).start()
    for r in range(1, NX):
        remote(outb.at[c, x], outb.at[c, x], ob_send.at[r - 1], ob_recv.at[r - 1], x_line(r)).start()
    out_copies = [pltpu.make_async_copy(outb.at[c, x], out_hbm.at[c, x], out_sem.at[0])]
    out_copies[-1].start()
    for r in range(NX - 1):
        drain(kx.at[0], kx_send.at[r])
        drain(ky.at[0], ky_send.at[r])
    for r in range(NZ - 1):
        drain(kz.at[0], kz_send.at[r])
    for i in range(NZ):
        drain(ys.at[0], ys_send.at[i])
    for i in range(1, NZ):
        drain(sbuf.at[0, pl.ds(0, NQ - 1)], rs_sem.at[i])
    def spread_out(r):
        xx = (x + NX - r) % NX
        drain(outb.at[0, 0], ob_recv.at[r - 1])
        remote(outb.at[c, xx], outb.at[c, xx], oc_send.at[r], oc_recv.at[r], core).start()
        out_copies.append(pltpu.make_async_copy(outb.at[c, xx], out_hbm.at[c, xx], out_sem.at[r]))
        out_copies[-1].start()

    def take_out(r):
        xx = (x + NX - r) % NX
        drain(outb.at[0, 0], oc_recv.at[r])
        out_copies.append(pltpu.make_async_copy(
            outb.at[1 - c, xx], out_hbm.at[1 - c, xx], out_sem.at[4 + r]))
        out_copies[-1].start()

    take_out(0)
    last_to_core()
    spread_out(1)
    spread_out(3)
    loss_and_rows()
    for copy in row_copies:
        copy.start()
    spread_out(2)
    for r in range(1, NX):
        take_out(r)

    for r in range(NX - 1):
        drain(outb.at[0, 0], ob_send.at[r])
    for r in range(NX):
        drain(outb.at[0, 0], oc_send.at[r])
    for i in range(1, NZ):
        drain(zbuf.at[0], ps_sem.at[i])
    drain(sbuf.at[0, pl.ds(0, NQ - 1)], rs_sem.at[0])
    for r in range(NZ - 1):
        drain(kz.at[0], lz_send.at[r])
    drain(lastz.at[0], lc_send)
    for copy in row_copies:
        copy.wait()
    for copy in out_copies:
        copy.wait()


def layer_call(tokens, ids, gates, positives, gate_up, down):
    tok, width = tokens.shape
    half = down.shape[0]
    ds = width // (NX * NC)
    hw = NX * ds
    rows = NY * SLOTS
    per = positives.shape[0]
    seqs = NZ * NY * per
    bf, f32 = jnp.bfloat16, jnp.float32
    dma = pltpu.SemaphoreType.DMA
    vm = pltpu.VMEM
    scratch = [
        vm((NZ, tok, ds), bf),
        vm((NX, tok, ds), bf),
        vm((NC, NX, 8, 128), f32),
        vm((24, tok), f32),
        vm((NZ, 16, tok), bf),
        vm((NZ, NQ, tok), f32),
        vm((NZ, NQ, tok), f32),
        vm((tok, tok), bf),
        vm((NZ, NQ, SLOTS, ds), bf),
        vm((NZ, rows, width), bf),
        vm((3, width, 2 * half // 3), bf),
        vm((NX * NC, half, ds), bf),
        vm((2 * rows, half), bf),
        vm((NZ, NX, rows, ds), bf),
        vm((NZ, NX, rows, ds), bf),
        vm((NZ, NX, rows, ds), bf),
        vm((NZ, NX, rows, ds), bf),
        vm((NZ, NQ, SLOTS, ds), bf),
        vm((7, tok, ds), bf),
        vm((NZ, tok, ds), bf),
        vm((2, tok, ds), f32),
        vm((NC, NX, tok, ds), bf),
        vm((NY, NY * per, hw), bf),
        vm((NY, NY * per, 128), f32),
        vm((NC, NZ, NY * per, hw), bf),
        vm((NZ, NY * per, 128), f32),
        vm((seqs, 2 * half), f32),
        vm((NZ, NY * per, hw), bf),
        vm((NZ, NY * per, hw), bf),
        vm((NZ, NY * per, hw), bf),
        vm((NZ, NY * per, hw), bf),
        vm((NZ, NY * per, hw), bf),
        vm((NY, NY * per, hw), bf),
        vm((NX, NY * per, hw), bf),
        vm((NC, NZ, NY * per, hw), bf),
        vm((width, seqs), bf),
        vm((half, seqs), bf),
        vm((seqs, width), bf),
        vm((seqs, 2 * half), bf),
        dma((20,)), dma((NZ,)), dma((7,)), dma((7,)),
        dma((7,)), dma((NZ,)), dma((7,)), dma((NZ,)),
        dma((NZ,)), dma((NZ,)), dma((NZ,)), dma((NZ,)), dma((NZ,)), dma((NZ,)),
        dma((NZ,)), dma((NZ,)), dma((NZ,)), dma((NZ,)), dma((NZ,)),
        dma((3,)), dma((3,)), dma((NX,)), dma((NX,)),
        dma((3,)), dma((3,)), dma((3,)), dma((3,)), dma((7,)), dma((NZ,)), dma((7,)), dma((NZ,)),
        dma, dma, dma, dma, dma((7,)), dma((7,)), dma((3,)), dma((3,)), dma((3,)), dma((3,)),
        dma((7,)), dma((7,)), dma, dma, dma((12,)),
    ]
    anyspec = pl.BlockSpec(memory_space=pl.ANY)
    vspec = pl.BlockSpec(memory_space=pltpu.VMEM)
    sspec = pl.BlockSpec(memory_space=pltpu.SMEM)
    return pl.pallas_call(
        layer_kernel,
        out_shape=(
            jax.ShapeDtypeStruct((NC, NX, tok, ds), bf),
            jax.ShapeDtypeStruct((width, seqs), bf),
            jax.ShapeDtypeStruct((half, seqs), bf),
            jax.ShapeDtypeStruct((seqs, width), bf),
            jax.ShapeDtypeStruct((seqs, 2 * half), bf),
        ),
        in_specs=[anyspec, vspec, vspec, sspec, anyspec, anyspec],
        out_specs=(anyspec,) * 5,
        scratch_shapes=scratch,
        compiler_params=pltpu.CompilerParams(
            collective_id=0, has_side_effects=True, vmem_limit_bytes=60 * 1024 * 1024),
        name="layer",
    )(tokens, ids, gates, positives, gate_up, down)


def finish_kernel(
    out_hbm, xlast_hbm, hid_hbm, rg_hbm, gp_hbm, layer_hbm, ggu_hbm, gd_hbm,
    out_v, xlast_v, hid_v, rg_v, gp_v, ggu_v, gd_v, in_sem, out_sem,
):
    tok, ds = out_v.shape[2], out_v.shape[3]
    reads = [
        pltpu.make_async_copy(src, dst, in_sem.at[n])
        for n, (src, dst) in enumerate((
            (gp_hbm, gp_v), (xlast_hbm, xlast_v), (rg_hbm, rg_v), (hid_hbm, hid_v),
            (out_hbm, out_v)))
    ]
    for read in reads:
        read.start()
    steps = NX * NC
    rows = xlast_v.shape[0] // steps
    hrows = hid_v.shape[0] // 3
    reads[0].wait()
    reads[1].wait()

    def ggu_out(n):
        part = pl.ds(pl.multiple_of(n * rows, rows), rows)
        return pltpu.make_async_copy(ggu_v.at[part], ggu_hbm.at[0, part], out_sem.at[n])

    @pl.loop(0, steps)
    def _(n):
        part = pl.ds(pl.multiple_of(n * rows, rows), rows)
        ggu_v[part] = jnp.dot(
            xlast_v[part], gp_v[...], preferred_element_type=jnp.float32).astype(jnp.bfloat16)
        ggu_out(n).start()

    for read in reads[2:]:
        read.wait()
    layer_out = [
        pltpu.make_async_copy(
            out_v.at[j % NC, j // NC], layer_hbm.at[:, pl.ds(j * ds, ds)], out_sem.at[steps + j])
        for j in range(steps)
    ]
    for copy in layer_out:
        copy.start()
    gd_out = []
    for n in range(3):
        part = pl.ds(n * hrows, hrows)
        gd_out.append(pltpu.make_async_copy(
            gd_v.at[part], gd_hbm.at[0, part], out_sem.at[2 * steps + n]))
        for j in range(steps // 2):
            cols = slice(2 * j * ds, 2 * (j + 1) * ds)
            gd_v[n * hrows:(n + 1) * hrows, cols] = jnp.dot(
                hid_v[part], rg_v[:, cols], preferred_element_type=jnp.float32
            ).astype(jnp.bfloat16)
        gd_out[-1].start()

    @pl.loop(0, steps)
    def _(n):
        ggu_out(n).wait()

    for copy in layer_out + gd_out:
        copy.wait()


def finish_call(out, xlast, hidden, route_grad, grad_projected):
    cores, xs, tok, ds = out.shape
    width, seqs = xlast.shape
    half = hidden.shape[0]
    bf = jnp.bfloat16
    anyspec = pl.BlockSpec(memory_space=pl.ANY)
    return pl.pallas_call(
        finish_kernel,
        in_specs=[anyspec] * 5,
        out_specs=(anyspec,) * 3,
        out_shape=(
            jax.ShapeDtypeStruct((tok, width), bf),
            jax.ShapeDtypeStruct((1, width, 2 * half), bf),
            jax.ShapeDtypeStruct((1, half, width), bf),
        ),
        scratch_shapes=[
            pltpu.VMEM(out.shape, bf),
            pltpu.VMEM(xlast.shape, bf),
            pltpu.VMEM(hidden.shape, bf),
            pltpu.VMEM(route_grad.shape, bf),
            pltpu.VMEM(grad_projected.shape, bf),
            pltpu.VMEM((width, 2 * half), bf),
            pltpu.VMEM((half, width), bf),
            pltpu.SemaphoreType.DMA((5,)),
            pltpu.SemaphoreType.DMA((2 * NX * NC + 3,)),
        ],
        compiler_params=pltpu.CompilerParams(vmem_limit_bytes=60 * 1024 * 1024),
        name="finish",
    )(out, xlast, hidden, route_grad, grad_projected)


def body(tokens, expert_ids, gates, positives, gate_up, down):
    return finish_call(*layer_call(
        tokens, expert_ids.reshape(2, -1), gates.reshape(2, -1), positives, gate_up[0], down[0]))


def solution(mesh):
    return jax.shard_map(
        body,
        mesh=mesh,
        in_specs=(
            P("dp", None),
            P("dp", "expert"),
            P("dp", "expert"),
            P("dp"),
            P(("dp", "expert"), None, None),
            P(("dp", "expert"), None, None),
        ),
        out_specs=(P("dp", None), P(("dp", "expert"), None, None), P(("dp", "expert"), None, None)),
        check_vma=False,
    )
```

```python
import functools

import jax
import jax.numpy as jnp
from jax import lax
from jax.experimental import pallas as pl
from jax.experimental.pallas import tpu as pltpu
from jax.sharding import PartitionSpec as P

logit_divisor = 0.05
grad_scale = 256.0
epsilon = 1e-06

MESH = pl.DeviceIdType.MESH
NZ, NY, NX, NC = 8, 4, 4, 2
NQ = NY * NX
SLOTS = 32


def layer_kernel(
    tok_hbm, ids_ref, gates_ref, pos_ref, gu_hbm, dn_hbm,
    out_hbm, xlast_hbm, hid_hbm, rg_hbm, gp_hbm,
    zbuf, tokc, mb, mo, mt, rk, gw, tri, sbuf, xm, gu, dn, hid, ys, yo, yr, rs, rbuf, prec, psend, pacc, outb,
    xly, mly, xlz, mlz, plast, kls, klo, klr, kz, kzr, ky, kx, lastp, lastz, hidl, xlast_ref, hid_ref, rg_ref, gp_ref,
    loc_sem, own_sem, mb_send, mb_recv, zs_sem, zr_sem, ms_sem, mr_sem,
    xs_sem, xr_sem, xf_send, xf_recv, ys_send, ys_recv, rs_sem, rr_sem, rown_sem, ps_sem, pr_sem,
    ob_send, ob_recv, oc_send, oc_recv,
    xly_send, xly_recv, mly_send, mly_recv, xlz_send, xlz_recv, mlz_send, mlz_recv,
    xlc_send, xlc_recv, klc_send, klc_recv, kz_send, kz_recv, ky_send, ky_recv, kx_send, kx_recv,
    lz_send, lz_recv, lc_send, lc_recv, ly_send, ly_recv, out_sem,
):
    dp = lax.axis_index("dp")
    ex = lax.axis_index("expert")
    z, y, x, c = dp // NY, dp % NY, ex // NC, ex % NC
    q_me = y * NX + x
    tok, ds = zbuf.shape[1], zbuf.shape[2]
    rows = NY * SLOTS
    hw = NX * ds
    seqs = plast.shape[0]
    per = seqs // (NZ * NY)
    length = tok // per
    core = (dp, x * NC + (1 - c))
    f32, bf = jnp.float32, jnp.bfloat16

    def at(zz, yy, xx):
        return (zz * NY + yy, xx * NC + c)

    def z_line(r):
        return at((z + r) % NZ, y, x)

    def y_line(r):
        return at(z, (y + r) % NY, x)

    def x_line(r):
        return at(z, y, (x + r) % NX)

    def group(r):
        return (dp, (ex + r) % (NX * NC))

    def plane(r):
        q = (q_me + r) % NQ
        return q, at(z, q // NX, q % NX)

    def plane_of(i):
        return (z + ((i + 1) // 2) * (2 * (i % 2) - 1) + NZ) % NZ

    def remote(src, dst, send, recv, device):
        return pltpu.make_async_remote_copy(
            src_ref=src, dst_ref=dst, send_sem=send, recv_sem=recv,
            device_id=device, device_id_type=MESH,
        )

    def drain(ref, sem):
        pltpu.make_async_copy(ref, ref, sem).wait()

    def signal(device):
        pl.semaphore_signal(barrier, inc=1, device_id=device, device_id_type=MESH)

    half = hid.shape[1]
    nch = gu.shape[0]
    ch = half // nch
    col_me = pl.multiple_of(ex * ds, ds)
    tok_load = pltpu.make_async_copy(tok_hbm.at[:, pl.ds(col_me, ds)], zbuf.at[0], loc_sem.at[0])
    tok_load.start()
    tok_loads = [
        pltpu.make_async_copy(
            tok_hbm.at[:, pl.ds(pl.multiple_of((xx * NC + c) * ds, ds), ds)], tokc.at[xx],
            loc_sem.at[1 + xx])
        for xx in range(NX)
    ]
    for load in tok_loads:
        load.start()
    loads = []
    for n in range(nch):
        for part in range(2):
            loads.append(pltpu.make_async_copy(
                gu_hbm.at[:, pl.ds(part * half + n * ch, ch)],
                gu.at[n, :, pl.ds(part * ch, ch)], loc_sem.at[5 + 2 * n + part]))
    for j in range(NX * NC):
        loads.append(pltpu.make_async_copy(
            dn_hbm.at[:, pl.ds(j * ds, ds)], dn.at[j], loc_sem.at[5 + 2 * nch + j]))

    for load in loads:
        load.start()

    barrier = pltpu.get_barrier_semaphore()

    @pl.loop(1, NZ)
    def _(r):
        signal(z_line(r))

    @pl.loop(1, NQ)
    def _(r):
        signal(plane(r)[1])

    signal(core)
    for r in range(1, NX):
        signal((dp, (x + r) % NX * NC + (1 - c)))

    lane = lax.broadcasted_iota(jnp.int32, (1, 128), 1)
    mb[c, x, 0:2, :] = ids_ref[...].astype(f32)
    mb[c, x, 2:4, :] = gates_ref[...]
    mb[c, x, 4:5, :] = jnp.where(lane < length, pos_ref[0], pos_ref[1]).astype(f32)
    mb[c, x, 5:6, :] = jnp.where(lane < length, pos_ref[2], pos_ref[3]).astype(f32)
    mb[c, x, 6:8, :] = jnp.zeros((2, 128), f32)
    ti = lax.broadcasted_iota(jnp.int32, (tok, tok), 0)
    tj = lax.broadcasted_iota(jnp.int32, (tok, tok), 1)
    tri[...] = jnp.where(ti < tj, 1.0, 0.0).astype(bf)

    lrow = lax.broadcasted_iota(jnp.int32, (NY * per, tok), 0)
    ltok = lax.broadcasted_iota(jnp.int32, (NY * per, tok), 1)
    last_sel = jnp.where(
        (ltok % length == length - 1) & (lrow == y * per + ltok // length), 1.0, 0.0)
    for load in tok_loads:
        load.wait()
    for xx in range(NX):
        xly[y, :, xx * ds:(xx + 1) * ds] = jnp.dot(
            last_sel.astype(bf), tokc[xx], preferred_element_type=f32).astype(bf)
    mly[y] = jnp.zeros((NY * per, 128), f32)
    tok_load.wait()
    pl.semaphore_wait(barrier, NZ + NQ - 1 + NX - 1)

    for r in range(1, NX * NC):
        remote(mb.at[c, x], mb.at[c, x], mb_send.at[r - 1], mb_recv.at[r - 1], group(r)).start()

    up, down = z_line(1), z_line(NZ - 1)

    def ring_own(view, down_view, up_view, send, recv):
        remote(view, down_view, send.at[6], recv.at[1], down).start()
        remote(view, up_view, send.at[0], recv.at[2], up).start()

    def ring_on(i, view, next_view, send, recv):
        device = at((z + 1 - 2 * (i % 2) + NZ) % NZ, y, x)
        remote(view, next_view, send.at[i], recv.at[i + 2], device).start()

    ring_own(zbuf.at[0], zbuf.at[1], zbuf.at[2], zs_sem, zr_sem)
    for r in range(1, NY):
        remote(xly.at[y], xly.at[y], xly_send.at[r - 1], xly_recv.at[r - 1], y_line(r)).start()

    for r in range(1, NX * NC):
        drain(mb.at[0, 0], mb_recv.at[r - 1])
    for side in range(2):
        cols = slice(side * 128, (side + 1) * 128)
        for part in range(2):
            for cc in range(NC):
                mo[part * 8 + cc * NX:part * 8 + (cc + 1) * NX, cols] = mb[cc, :, 2 * part + side, :]
        mo[16:24, cols] = jnp.broadcast_to(mb[0, 0, 4 + side:5 + side, :], (8, 128))
    mt[0] = mo[0:16, :].astype(bf)
    ring_own(mt.at[0], mt.at[1], mt.at[2], ms_sem, mr_sem)

    slot_iota = lax.broadcasted_iota(jnp.int32, (SLOTS, tok), 0).astype(f32)

    def gather_block(i):
        table = mt[i].astype(f32)
        ids, gate = table[0:8], table[8:16]
        hits, weights = [], []
        for q in range(NQ):
            hit = ids == (z * NQ + q).astype(f32)
            hits.append(jnp.sum(jnp.where(hit, 1.0, 0.0), axis=0, keepdims=True))
            weights.append(jnp.sum(jnp.where(hit, gate, 0.0), axis=0, keepdims=True))
        hit = jnp.concatenate(hits, axis=0)
        rank = jnp.dot(hit.astype(bf), tri[...], preferred_element_type=f32)
        ranked = jnp.where(hit > 0.0, rank, -1.0)
        rk[i] = ranked
        gw[i] = jnp.concatenate(weights, axis=0)
        picks = jnp.concatenate(
            [jnp.where(slot_iota == ranked[q:q + 1, :], 1.0, 0.0) for q in range(NQ)], axis=0
        ).astype(bf)
        got = jnp.dot(picks, zbuf[i], preferred_element_type=f32)
        sbuf[i] = got.astype(bf).reshape(NQ, SLOTS, ds)

        def place():
            return xm.at[i, pl.ds(pl.multiple_of(y * SLOTS, SLOTS), SLOTS), pl.ds(col_me, ds)]

        @pl.loop(1, NQ)
        def _(r):
            q, device = plane(r)
            remote(sbuf.at[i, q], place(), xs_sem.at[i], xr_sem.at[i], device).start()

        pltpu.make_async_copy(sbuf.at[i, q_me], place(), own_sem.at[i]).start()

    gather_block(0)

    mly[y, :, 0:24] = lax.dot_general(
        last_sel, mo[...], (((1,), (1,)), ((), ())), precision=lax.Precision.HIGHEST,
        preferred_element_type=f32)
    for r in range(1, NY):
        remote(mly.at[y], mly.at[y], mly_send.at[r - 1], mly_recv.at[r - 1], y_line(r)).start()
    def last_rows_own():
        for r in range(1, NY):
            drain(xly.at[0], xly_recv.at[r - 1])
        total = xly[0].astype(f32)
        for r in range(1, NY):
            total += xly[r].astype(f32)
        xlz[c, z] = total.astype(bf)
        for r in range(1, NY):
            drain(mly.at[0], mly_recv.at[r - 1])
        mlz[z] = mly[0] + mly[1] + mly[2] + mly[3]
        for r in range(1, NZ):
            remote(xlz.at[c, z], xlz.at[c, z], xlz_send.at[r - 1], xlz_recv.at[r - 1],
                   z_line(r)).start()
            remote(mlz.at[z], mlz.at[z], mlz_send.at[r - 1], mlz_recv.at[r - 1], z_line(r)).start()

    def forward(i):
        drain(sbuf.at[0, pl.ds(0, NQ - 1)], xr_sem.at[i])
        drain(sbuf.at[0, 0], own_sem.at[i])
        for xx in range(NX):
            cols = pl.ds(pl.multiple_of((xx * NC + c) * ds, ds), ds)
            remote(xm.at[i, :, cols], xm.at[i, :, cols], xf_send.at[i], xf_recv.at[i], core).start()

    def silu_mul(pr):
        g, u = pr[:, :ch], pr[:, ch:]
        return (g * jax.nn.sigmoid(g) * u).astype(bf)

    def experts(p):
        for b in range(2):
            drain(xm.at[0, :, pl.ds(0, hw)], xf_recv.at[2 * p + b])
        xrows = xm[pl.ds(2 * p, 2)].reshape(2 * rows, NC * hw)
        for n in range(nch):
            hid[:, n * ch:(n + 1) * ch] = silu_mul(
                jnp.dot(xrows, gu[n], preferred_element_type=f32))
        hv = hid[...]
        for xx in range(NX):
            o = jnp.dot(hv, dn[xx * NC + 1 - c], preferred_element_type=f32).astype(bf)
            ys[2 * p, xx] = o[:rows]
            ys[2 * p + 1, xx] = o[rows:]
        for b in range(2):
            remote(ys.at[2 * p + b], yr.at[2 * p + b], ys_send.at[2 * p + b],
                   ys_recv.at[2 * p + b], core).start()
        for xx in range(NX):
            o = jnp.dot(hv, dn[xx * NC + c], preferred_element_type=f32).astype(bf)
            yo[2 * p, xx] = o[:rows]
            yo[2 * p + 1, xx] = o[rows:]

    def all_columns(buf, j):
        part = buf[j % NC, :, :, (j // NC) * ds:(j // NC + 1) * ds]
        return part.reshape(seqs, ds)

    def experts_last():
        drain(xlz.at[0], xlc_recv)
        xrows = jnp.concatenate([all_columns(xlz, j) for j in range(NX * NC)], axis=1)
        for n in range(nch):
            pr = jnp.dot(xrows, gu[n], preferred_element_type=f32)
            plast[:, 2 * n * ch:2 * (n + 1) * ch] = pr
            hid[:seqs, n * ch:(n + 1) * ch] = silu_mul(pr)
        hv = hid[:seqs]
        hidl[...] = hv
        for xx in range(NX):
            o = jnp.dot(hv, dn[xx * NC + 1 - c], preferred_element_type=f32).astype(bf)
            kls[:, :, xx * ds:(xx + 1) * ds] = o.reshape(NZ, NY * per, ds)
        remote(kls, klr, klc_send, klc_recv, core).start()
        for xx in range(NX):
            o = jnp.dot(hv, dn[xx * NC + c], preferred_element_type=f32).astype(bf)
            klo[:, :, xx * ds:(xx + 1) * ds] = o.reshape(NZ, NY * per, ds)

    lanes = lax.broadcasted_iota(jnp.int32, (seqs, 128), 1)

    def last_weight():
        m = mlz[...].reshape(seqs, 128)
        mine = (m == (dp * NX + x).astype(f32)) & (lanes < 8)
        return jnp.sum(jnp.where(mine, pltpu.roll(m, 120, 1), 0.0), axis=1, keepdims=True)

    def last_to_planes():
        drain(klr, klc_recv)
        both = klo[...].astype(f32) + klr[...].astype(f32)
        kz[...] = (both.reshape(seqs, hw) * last_weight()).astype(bf).reshape(NZ, NY * per, hw)
        for r in range(1, NZ):
            remote(kz.at[(z + r) % NZ], kzr.at[z], kz_send.at[r - 1], kz_recv.at[r - 1],
                   z_line(r)).start()

    def last_to_y():
        for r in range(1, NZ):
            drain(kz.at[0], kz_recv.at[r - 1])
        total = kz[z].astype(f32)
        for r in range(1, NZ):
            total += kzr[(z + r) % NZ].astype(f32)
        ky[y] = total.astype(bf)
        for r in range(1, NY):
            remote(ky.at[y], ky.at[y], ky_send.at[r - 1], ky_recv.at[r - 1], y_line(r)).start()

    def last_to_x():
        for r in range(1, NY):
            drain(ky.at[0], ky_recv.at[r - 1])
        total = ky[0].astype(f32)
        for r in range(1, NY):
            total += ky[r].astype(f32)
        kx[x] = total.astype(bf)
        for r in range(1, NX):
            remote(kx.at[x], kx.at[x], kx_send.at[r - 1], kx_recv.at[r - 1], x_line(r)).start()

    def last_to_all():
        for r in range(1, NX):
            drain(kx.at[0], kx_recv.at[r - 1])
        total = kx[0].astype(f32)
        for r in range(1, NX):
            total += kx[r].astype(f32)
        last = (xlz[c, z].astype(f32) + total).astype(bf)
        for k in range(NX):
            lastp[k] = last[:, k * ds:(k + 1) * ds]
        lastz[c, y, z] = lastp[y]
        for r in range(1, NZ):
            remote(lastz.at[c, y, z], lastz.at[c, y, z], lz_send.at[r - 1], lz_recv.at[r - 1],
                   z_line(r)).start()

    def last_to_rows():
        for r in range(1, NZ):
            drain(lastp.at[0], lz_recv.at[r - 1])
        for r in range(1, NY):
            remote(lastz.at[c, y], lastz.at[c, y], ly_send.at[r - 1], ly_recv.at[r - 1],
                   y_line(r)).start()

    def last_to_core():
        for r in range(1, NY):
            drain(lastz.at[0, 0], ly_recv.at[r - 1])
        remote(lastz.at[c], lastz.at[c], lc_send, lc_recv, core).start()

    def loss_and_rows():
        drain(lastz.at[0], lc_recv)
        dots = jnp.zeros((seqs, seqs), f32)
        for j in range(NX * NC):
            part = lastz[j % NC, j // NC].reshape(seqs, ds)
            dots += lax.dot_general(
                part, part, (((1,), (1,)), ((), ())), preferred_element_type=f32)
        ri = lax.broadcasted_iota(jnp.int32, (seqs, seqs), 0)
        cj = lax.broadcasted_iota(jnp.int32, (seqs, seqs), 1)
        eye = ri == cj
        squares = jnp.where(eye, dots, 0.0)
        n_col = jnp.sqrt(jnp.sum(squares, axis=1, keepdims=True) + epsilon)
        n_row = jnp.sqrt(jnp.sum(squares, axis=0, keepdims=True) + epsilon)
        scores = dots / (n_col * n_row) / logit_divisor
        exps = jnp.where(eye, 0.0, jnp.exp(scores))
        prob = exps / jnp.sum(exps, axis=1, keepdims=True)
        m = mlz[...].reshape(seqs, 128)
        positive = jnp.sum(jnp.where(lanes == 16, m, 0.0), axis=1, keepdims=True)
        coef = grad_scale * (prob - jnp.where(cj.astype(f32) == positive, 1.0, 0.0))
        both = coef + coef.T
        proj = jnp.sum(both * scores, axis=1, keepdims=True)
        mat = (both / (n_row * logit_divisor) - jnp.where(eye, proj / n_col, 0.0)) / n_col
        mat = mat * last_weight()
        first = mat.astype(bf)
        second = (mat - first.astype(f32)).astype(bf)
        grad_hidden = jnp.zeros((seqs, half), f32)
        for j in range(NX * NC):
            lj = lastz[j % NC, j // NC].reshape(seqs, ds)
            g = jnp.dot(first, lj, preferred_element_type=f32)
            g += jnp.dot(second, lj, preferred_element_type=f32)
            g = g.astype(bf)
            rg_ref[:, j * ds:(j + 1) * ds] = g
            grad_hidden += lax.dot_general(
                g, dn[j], (((1,), (1,)), ((), ())), preferred_element_type=f32)
        for n in range(nch):
            gate_part = plast[:, 2 * n * ch:(2 * n + 1) * ch]
            up_part = plast[:, (2 * n + 1) * ch:2 * (n + 1) * ch]
            gh = grad_hidden[:, n * ch:(n + 1) * ch]
            sig = jax.nn.sigmoid(gate_part)
            gp_ref[:, n * ch:(n + 1) * ch] = (
                gh * up_part * (sig * (1.0 + gate_part * (1.0 - sig)))).astype(bf)
            gp_ref[:, half + n * ch:half + (n + 1) * ch] = (gh * (gate_part * sig)).astype(bf)

    def swap_last_rows():
        for r in range(NZ - 1):
            drain(xlz.at[0, 0], xlz_recv.at[r])
            drain(mlz.at[0], mlz_recv.at[r])
        remote(xlz.at[c], xlz.at[c], xlc_send, xlc_recv, core).start()

    def send_back(i):
        drain(ys.at[0], ys_recv.at[i])
        rs[i] = (yo[i].astype(f32) + yr[i].astype(f32)).astype(bf)

        def piece(q):
            return rs.at[i, q % NX, pl.ds(pl.multiple_of((q // NX) * SLOTS, SLOTS), SLOTS)]

        @pl.loop(1, NQ)
        def _(r):
            q, device = plane(r)
            remote(piece(q), rbuf.at[i, q_me], rs_sem.at[i], rr_sem.at[i], device).start()

        pltpu.make_async_copy(piece(q_me), rbuf.at[i, q_me], rown_sem.at[i]).start()

    @pl.loop(1, 11)
    def _(i):
        @pl.when((i == 7) | (i == 9) | (i == 10))
        def _():
            experts((i - 7) // 2 + (i // 10))

        @pl.when(i < NZ)
        def _():
            drain(zbuf.at[0], zr_sem.at[i])
            drain(mt.at[0], mr_sem.at[i])

            @pl.when(i <= 5)
            def _():
                ring_on(i, zbuf.at[i], zbuf.at[i + 2], zs_sem, zr_sem)
                ring_on(i, mt.at[i], mt.at[i + 2], ms_sem, mr_sem)

            gather_block(i)

        @pl.when(i >= 5)
        def _():
            forward(i - 5 + (i + 1) // 8 + i // 10)

        @pl.when((i == 6) | (i == 9))
        def _():
            forward(2 + 4 * (i // 9))

        @pl.when(i == 5)
        def _():
            for load in loads:
                load.wait()

        @pl.when(i == 6)
        def _():
            last_rows_own()

        @pl.when(i == 9)
        def _():
            swap_last_rows()

    experts_last()
    send_back(5)
    send_back(4)
    last_to_planes()
    experts(NZ // 2 - 1)

    def arrived(i):
        drain(sbuf.at[0, pl.ds(0, NQ - 1)], rr_sem.at[i])
        drain(sbuf.at[0, 0], rown_sem.at[i])

    def combine(i):
        ranked, w = rk[i], gw[i]
        spread = jnp.concatenate(
            [jnp.where(slot_iota == ranked[q:q + 1, :], w[q:q + 1, :], 0.0) for q in range(NQ)],
            axis=0,
        ).astype(bf)
        return lax.dot_general(
            spread, rbuf[i].reshape(NQ * SLOTS, ds), (((0,), (0,)), ((), ())),
            preferred_element_type=f32)


    row_copies = [
        pltpu.make_async_copy(src, dst, out_sem.at[8 + n]) for n, (src, dst) in enumerate((
            (xlast_ref, xlast_hbm), (hid_ref, hid_hbm), (rg_ref, rg_hbm), (gp_ref, gp_hbm)))]

    def drained_early():
        for r in range(NX * NC - 1):
            drain(mb.at[0, 0], mb_send.at[r])
        for r in range(NY - 1):
            drain(xly.at[0], xly_send.at[r])
            drain(mly.at[0], mly_send.at[r])
        for r in range(NZ - 1):
            drain(zbuf.at[0], zs_sem.at[r])
            drain(mt.at[0], ms_sem.at[r])
            drain(xlz.at[0, 0], xlz_send.at[r])
            drain(mlz.at[0], mlz_send.at[r])
        drain(xlz.at[0], xlc_send)
        drain(kls, klc_send)
        for n in range(NZ):
            drain(sbuf.at[0, pl.ds(0, NQ - 1)], xs_sem.at[n])
            drain(xm.at[0, :, pl.ds(0, hw)], xf_send.at[n])

    def order(n):
        return NZ - 1 - n + (1 - n // 4) * (4 * (n // 2 % 2) - 2)

    def sum_on(i):
        slot = (i + 5) % 7
        device = at((z - 1 + 2 * (i % 2) + NZ) % NZ, y, x)
        remote(psend.at[i], prec.at[slot], ps_sem.at[i], pr_sem.at[slot], device).start()

    def add_on(i):
        drain(prec.at[0], pr_sem.at[i])
        psend[i] = (pacc[i - 4] + prec[i].astype(f32)).astype(bf)
        sum_on(i)

    @pl.loop(0, NZ - 1)
    def _(n):
        i = order(n)
        arrived(i)

        @pl.when(n <= NZ - 3)
        def _():
            send_back(order(n + 2))

        part = combine(i)

        @pl.when((n >= 2) & (n < 4))
        def _():
            psend[i] = part.astype(bf)
            sum_on(i)

        @pl.when(n < 2)
        def _():
            pacc[i - 4] = part

        @pl.when(n == 3)
        def _():
            add_on(5)

        @pl.when(n == 4)
        def _():
            add_on(4)

        @pl.when(n >= 4)
        def _():
            drain(prec.at[0], pr_sem.at[i])
            psend[i] = (part + prec[i].astype(f32)).astype(bf)
            sum_on(i)

        @pl.when(n == 0)
        def _():
            drained_early()

        @pl.when(n == 1)
        def _():
            last_to_y()

        @pl.when(n == 2)
        def _():
            hid_ref[...] = hidl[...].astype(f32).T.astype(bf)
            for j in range(NX * NC):
                xlast_ref[j * ds:(j + 1) * ds, :] = all_columns(xlz, j).astype(f32).T.astype(bf)
            row_copies[0].start()
            row_copies[1].start()

        @pl.when(n == 3)
        def _():
            last_to_x()

        @pl.when(n == 5)
        def _():
            last_to_all()

    last_to_rows()
    arrived(0)
    part = combine(0)
    drain(prec.at[0], pr_sem.at[0])
    drain(prec.at[0], pr_sem.at[6])
    part += prec[0].astype(f32) + prec[6].astype(f32)
    outb[c, x] = (zbuf[0].astype(f32) + part).astype(bf)
    remote(outb.at[c, x], outb.at[c, x], oc_send.at[0], oc_recv.at[0], core).start()
    for r in range(1, NX):
        remote(outb.at[c, x], outb.at[c, x], ob_send.at[r - 1], ob_recv.at[r - 1], x_line(r)).start()
    out_copies = [pltpu.make_async_copy(outb.at[c, x], out_hbm.at[c, x], out_sem.at[0])]
    out_copies[-1].start()
    for r in range(NX - 1):
        drain(kx.at[0], kx_send.at[r])
        drain(ky.at[0], ky_send.at[r])
    for r in range(NZ - 1):
        drain(kz.at[0], kz_send.at[r])
    for i in range(NZ):
        drain(ys.at[0], ys_send.at[i])
    for i in range(1, NZ):
        drain(sbuf.at[0, pl.ds(0, NQ - 1)], rs_sem.at[i])
    def spread_out(r):
        xx = (x + NX - r) % NX
        drain(outb.at[0, 0], ob_recv.at[r - 1])
        remote(outb.at[c, xx], outb.at[c, xx], oc_send.at[r], oc_recv.at[r], core).start()
        out_copies.append(pltpu.make_async_copy(outb.at[c, xx], out_hbm.at[c, xx], out_sem.at[r]))
        out_copies[-1].start()

    def take_out(r):
        xx = (x + NX - r) % NX
        drain(outb.at[0, 0], oc_recv.at[r])
        out_copies.append(pltpu.make_async_copy(
            outb.at[1 - c, xx], out_hbm.at[1 - c, xx], out_sem.at[4 + r]))
        out_copies[-1].start()

    for i in range(1, NZ):
        drain(zbuf.at[0], ps_sem.at[i])
    last_to_core()
    spread_out(1)
    spread_out(3)
    spread_out(2)
    loss_and_rows()
    for copy in row_copies[2:]:
        copy.start()
    for r in range(NX):
        take_out(r)

    for r in range(NX - 1):
        drain(outb.at[0, 0], ob_send.at[r])
    for r in range(NX):
        drain(outb.at[0, 0], oc_send.at[r])
    drain(sbuf.at[0, pl.ds(0, NQ - 1)], rs_sem.at[0])
    for r in range(NZ - 1):
        drain(lastp.at[0], lz_send.at[r])
    for r in range(NY - 1):
        drain(lastz.at[0, 0], ly_send.at[r])
    drain(lastz.at[0], lc_send)
    for copy in row_copies:
        copy.wait()
    for copy in out_copies:
        copy.wait()


def layer_call(tokens, ids, gates, positives, gate_up, down):
    tok, width = tokens.shape
    half = down.shape[0]
    ds = width // (NX * NC)
    hw = NX * ds
    rows = NY * SLOTS
    per = positives.shape[0]
    seqs = NZ * NY * per
    bf, f32 = jnp.bfloat16, jnp.float32
    dma = pltpu.SemaphoreType.DMA
    vm = pltpu.VMEM
    scratch = [
        vm((NZ, tok, ds), bf),
        vm((NX, tok, ds), bf),
        vm((NC, NX, 8, 128), f32),
        vm((24, tok), f32),
        vm((NZ, 16, tok), bf),
        vm((NZ, NQ, tok), f32),
        vm((NZ, NQ, tok), f32),
        vm((tok, tok), bf),
        vm((NZ, NQ, SLOTS, ds), bf),
        vm((NZ, rows, width), bf),
        vm((3, width, 2 * half // 3), bf),
        vm((NX * NC, half, ds), bf),
        vm((2 * rows, half), bf),
        vm((NZ, NX, rows, ds), bf),
        vm((NZ, NX, rows, ds), bf),
        vm((NZ, NX, rows, ds), bf),
        vm((NZ, NX, rows, ds), bf),
        vm((NZ, NQ, SLOTS, ds), bf),
        vm((7, tok, ds), bf),
        vm((NZ, tok, ds), bf),
        vm((2, tok, ds), f32),
        vm((NC, NX, tok, ds), bf),
        vm((NY, NY * per, hw), bf),
        vm((NY, NY * per, 128), f32),
        vm((NC, NZ, NY * per, hw), bf),
        vm((NZ, NY * per, 128), f32),
        vm((seqs, 2 * half), f32),
        vm((NZ, NY * per, hw), bf),
        vm((NZ, NY * per, hw), bf),
        vm((NZ, NY * per, hw), bf),
        vm((NZ, NY * per, hw), bf),
        vm((NZ, NY * per, hw), bf),
        vm((NY, NY * per, hw), bf),
        vm((NX, NY * per, hw), bf),
        vm((NX, NY * per, ds), bf),
        vm((NC, NY, NZ, NY * per, ds), bf),
        vm((seqs, half), bf),
        vm((width, seqs), bf),
        vm((half, seqs), bf),
        vm((seqs, width), bf),
        vm((seqs, 2 * half), bf),
        dma((20,)), dma((NZ,)), dma((7,)), dma((7,)),
        dma((7,)), dma((NZ,)), dma((7,)), dma((NZ,)),
        dma((NZ,)), dma((NZ,)), dma((NZ,)), dma((NZ,)), dma((NZ,)), dma((NZ,)),
        dma((NZ,)), dma((NZ,)), dma((NZ,)), dma((NZ,)), dma((NZ,)),
        dma((3,)), dma((3,)), dma((NX,)), dma((NX,)),
        dma((3,)), dma((3,)), dma((3,)), dma((3,)), dma((7,)), dma((NZ,)), dma((7,)), dma((NZ,)),
        dma, dma, dma, dma, dma((7,)), dma((7,)), dma((3,)), dma((3,)), dma((3,)), dma((3,)),
        dma((7,)), dma((7,)), dma, dma, dma((3,)), dma((3,)), dma((12,)),
    ]
    anyspec = pl.BlockSpec(memory_space=pl.ANY)
    vspec = pl.BlockSpec(memory_space=pltpu.VMEM)
    sspec = pl.BlockSpec(memory_space=pltpu.SMEM)
    hspec = pl.BlockSpec(memory_space=pltpu.HBM)
    return pl.pallas_call(
        layer_kernel,
        out_shape=(
            jax.ShapeDtypeStruct((NC, NX, tok, ds), bf),
            jax.ShapeDtypeStruct((width, seqs), bf),
            jax.ShapeDtypeStruct((half, seqs), bf),
            jax.ShapeDtypeStruct((seqs, width), bf),
            jax.ShapeDtypeStruct((seqs, 2 * half), bf),
        ),
        in_specs=[hspec, vspec, vspec, sspec, hspec, hspec],
        out_specs=(anyspec,) * 5,
        scratch_shapes=scratch,
        compiler_params=pltpu.CompilerParams(
            collective_id=0, has_side_effects=True, vmem_limit_bytes=40 * 1024 * 1024),
        name="layer",
    )(tokens, ids, gates, positives, gate_up, down)


def finish_kernel(
    out_hbm, xlast_hbm, hid_hbm, rg_hbm, gp_hbm, layer_hbm, ggu_hbm, gd_hbm,
    out_v, xlast_v, hid_v, rg_v, gp_v, ggu_v, gd_v, in_sem, out_sem,
):
    tok, ds = out_v.shape[2], out_v.shape[3]
    reads = [
        pltpu.make_async_copy(src, dst, in_sem.at[n])
        for n, (src, dst) in enumerate((
            (gp_hbm, gp_v), (xlast_hbm, xlast_v), (rg_hbm, rg_v), (hid_hbm, hid_v),
            (out_hbm, out_v)))
    ]
    for read in reads:
        read.start()
    steps = NX * NC
    rows = xlast_v.shape[0] // steps
    hrows = hid_v.shape[0] // 3
    reads[0].wait()
    reads[1].wait()

    def ggu_out(n):
        part = pl.ds(pl.multiple_of(n * rows, rows), rows)
        return pltpu.make_async_copy(ggu_v.at[part], ggu_hbm.at[0, part], out_sem.at[n])

    @pl.loop(0, steps)
    def _(n):
        part = pl.ds(pl.multiple_of(n * rows, rows), rows)
        ggu_v[part] = jnp.dot(
            xlast_v[part], gp_v[...], preferred_element_type=jnp.float32).astype(jnp.bfloat16)
        ggu_out(n).start()

    for read in reads[2:]:
        read.wait()
    layer_out = [
        pltpu.make_async_copy(
            out_v.at[j % NC, j // NC], layer_hbm.at[:, pl.ds(j * ds, ds)], out_sem.at[steps + j])
        for j in range(steps)
    ]
    for copy in layer_out:
        copy.start()
    gd_out = []
    for n in range(3):
        part = pl.ds(n * hrows, hrows)
        gd_out.append(pltpu.make_async_copy(
            gd_v.at[part], gd_hbm.at[0, part], out_sem.at[2 * steps + n]))
        for j in range(steps // 2):
            cols = slice(2 * j * ds, 2 * (j + 1) * ds)
            gd_v[n * hrows:(n + 1) * hrows, cols] = jnp.dot(
                hid_v[part], rg_v[:, cols], preferred_element_type=jnp.float32
            ).astype(jnp.bfloat16)
        gd_out[-1].start()

    @pl.loop(0, steps)
    def _(n):
        ggu_out(n).wait()

    for copy in layer_out + gd_out:
        copy.wait()


def finish_call(out, xlast, hidden, route_grad, grad_projected):
    cores, xs, tok, ds = out.shape
    width, seqs = xlast.shape
    half = hidden.shape[0]
    bf = jnp.bfloat16
    anyspec = pl.BlockSpec(memory_space=pl.ANY)
    return pl.pallas_call(
        finish_kernel,
        in_specs=[anyspec] * 5,
        out_specs=(anyspec,) * 3,
        out_shape=(
            jax.ShapeDtypeStruct((tok, width), bf),
            jax.ShapeDtypeStruct((1, width, 2 * half), bf),
            jax.ShapeDtypeStruct((1, half, width), bf),
        ),
        scratch_shapes=[
            pltpu.VMEM(out.shape, bf),
            pltpu.VMEM(xlast.shape, bf),
            pltpu.VMEM(hidden.shape, bf),
            pltpu.VMEM(route_grad.shape, bf),
            pltpu.VMEM(grad_projected.shape, bf),
            pltpu.VMEM((width, 2 * half), bf),
            pltpu.VMEM((half, width), bf),
            pltpu.SemaphoreType.DMA((5,)),
            pltpu.SemaphoreType.DMA((2 * NX * NC + 3,)),
        ],
        compiler_params=pltpu.CompilerParams(vmem_limit_bytes=12 * 1024 * 1024),
        name="finish",
    )(out, xlast, hidden, route_grad, grad_projected)


def body(tokens, expert_ids, gates, positives, gate_up, down):
    tokens, ids, weights, weight_in, weight_out = (
        pltpu.with_memory_space_constraint(v, pltpu.HBM) for v in (
            tokens, expert_ids.reshape(2, -1), gates.reshape(2, -1), gate_up[0], down[0]))
    return finish_call(*layer_call(
        tokens, ids, weights, positives, weight_in, weight_out))


def solution(mesh):
    return jax.shard_map(
        body,
        mesh=mesh,
        in_specs=(
            P("dp", None),
            P("dp", "expert"),
            P("dp", "expert"),
            P("dp"),
            P(("dp", "expert"), None, None),
            P(("dp", "expert"), None, None),
        ),
        out_specs=(P("dp", None), P(("dp", "expert"), None, None), P(("dp", "expert"), None, None)),
        check_vma=False,
    )
```
